512 devices in a mesh: pole: 8 (over y_hi, core), sep: 64 (over y_lo, z, x).
Axes of the slice: x: 4, y: 8 (y_hi: 4, y_lo: 2; y = y_hi * 2 + y_lo), z: 8, core: 2. Of those that a mesh axis runs over, the one named last changes fastest.
Arguments:
- diag_inverse: bfloat16 [8, 512, 2, 256, 256], P('pole', 'sep'), may hold values from -6 to 6
- coupling: bfloat16 [8, 512, 2, 256, 256], P('pole', 'sep'), may hold values from -0.25 to 0.25
- ancestor_inverse: bfloat16 [8, 64, 2, 256, 256], P('pole', 'sep'), may hold values from -6 to 6
- pole_weight: float32 [8, 2], P('pole'), may hold values from -1 to 1
- ancestor_bit: int32 [512], P('sep'), may hold values from 0 to 3
- tile_blocks: int32 [64, 6], P('sep'), may hold values from 0 to 511, as said below
- tile_count: int32 [64], P('sep'), may hold values from 1 to 6
- orbital_values: bfloat16 [64, 6, 2048, 256], P('sep', None, 'pole'), may hold values from -0.375 to 0.375
Outputs:
- density_grid: float32 [64, 2048], P('sep', 'pole')
The draws below stay inside these ranges and needn't reach their ends.
Inputs may be any that keep to these rules, and one draw needn't show every extreme that they name: `tile_blocks`: entry (t, s) names a block owned by device t - 1, t or t + 1 of sep, block b being owned by device b // 8.
All inputs are finite; a program needn't handle non-finite values.
Results may differ from the reference program's by a relative error of at most 0.0035.
Values may be sent and summed in bfloat16 or wider, within the bound.
No kernel may reach another device: no remote copies, remote signals or barrier semaphores. Data moves between devices by JAX's collectives and lax.ppermute only.
A program may use at most 64 MiB of HBM per device.

```python
import jax
import jax.numpy as jnp
from jax import lax

W = 256
B_DEV = 8
SLOTS = 6
LEVELS = 4
POLES = 8
NBLK = 512
NTILES = 64
PTS = 2048
N_SEP = 64


def draw_tile_blocks(key, part):
    first, second = jax.random.split(jax.random.fold_in(key, 7))
    tile = jnp.arange(NTILES, dtype=jnp.int32)[:, None]
    offset = jax.random.randint(first, (NTILES, SLOTS), -1, 2, dtype=jnp.int32)
    device = jnp.clip(tile + offset, 0, NTILES - 1)
    local = jax.random.randint(second, (NTILES, SLOTS), 0, B_DEV, dtype=jnp.int32)
    return (device * B_DEV + local).astype(jnp.int32)


def touch_ends(array, stream_key, low, high):
    extent = array.shape
    spot = [jax.random.randint(jax.random.fold_in(stream_key, axis), (), 0, extent[axis]) for axis in range(len(extent))]
    array = array.at[tuple(spot)].set(low)
    longest = extent.index(max(extent))
    spot[longest] = (spot[longest] + 1) % extent[longest]
    return array.at[tuple(spot)].set(high)


def steps_of(key, extent, shards, low, high):
    level, own = 1.0, jax.random.fold_in(key, 6)
    for dim, shards_of in shards:
        heights = jnp.exp(jax.random.uniform(jax.random.fold_in(own, dim), (shards_of,), jnp.float32, low / len(shards), high / len(shards)))
        level = level * jnp.repeat(heights, extent[dim] // shards_of).reshape([-1 if axis == dim else 1 for axis in range(len(extent))])
    return level


def scatter_about(stream_key, dims, deviation, reach, pieces=(), kind=jnp.bfloat16):
    loudness = steps_of(stream_key, dims, pieces, -0.22, 0.18) if pieces else 1.0
    array = jax.random.normal(stream_key, dims, jnp.float32) * deviation * loudness
    return jnp.minimum(jnp.maximum(array, -reach), reach).astype(kind)


def setup_inputs(seed: int = 0) -> dict:
    streams_of = jax.random.split(jax.random.key(seed), 9)
    diag_inverse = scatter_about(streams_of[0], (POLES, NBLK, 2, W, W), 1.0, 6.0, ((0, 8), (1, 64)))
    coupling = scatter_about(streams_of[1], (POLES, NBLK, 2, W, W), (2 * W) ** -0.5, 0.25, ((0, 8), (1, 64)))
    ancestor_inverse = scatter_about(streams_of[2], (POLES, N_SEP, 2, W, W), 1.0, 6.0, ((0, 8), (1, 64)))
    pole_weight = jnp.clip(jax.random.uniform(streams_of[3], (POLES, 2), jnp.float32, -1.0, 1.0) * steps_of(streams_of[3], (POLES, 2), ((0, 8),), -0.4, 0.0), -1.0, 1.0)
    ancestor_bit = touch_ends(jax.random.randint(streams_of[4], (NBLK,), 0, LEVELS), jax.random.fold_in(streams_of[4], 1), 0, LEVELS - 1).astype(jnp.int32)
    tile_blocks = draw_tile_blocks(jax.random.fold_in(streams_of[8], 71), 0)
    tile_count = touch_ends(jax.random.randint(streams_of[6], (NTILES,), 1, SLOTS + 1), jax.random.fold_in(streams_of[6], 1), 1, SLOTS).astype(jnp.int32)
    orbital_values = scatter_about(streams_of[7], (NTILES, SLOTS, PTS, W), W ** -0.5, 0.375, ((0, 64), (2, 8)))
    return dict(diag_inverse=diag_inverse, coupling=coupling, ancestor_inverse=ancestor_inverse, pole_weight=pole_weight, ancestor_bit=ancestor_bit, tile_blocks=tile_blocks, tile_count=tile_count, orbital_values=orbital_values)


def product(left, right):
    return jnp.einsum("pij,pjk->pik", left, right, precision=lax.Precision.HIGHEST)


def product_t(left, right):
    return jnp.einsum("pij,pkj->pik", left, right, precision=lax.Precision.HIGHEST)


def reference(diag_inverse, coupling, ancestor_inverse, pole_weight, ancestor_bit, tile_blocks, tile_count, orbital_values):
    block_ids = jnp.arange(NBLK, dtype=jnp.int32)
    owner = jnp.bitwise_xor(block_ids // B_DEV, jnp.left_shift(jnp.ones_like(ancestor_bit), ancestor_bit)).astype(jnp.int32)

    def one_block(index):
        link = coupling[:, index].astype(jnp.float32)
        upper = ancestor_inverse[:, owner[index]].astype(jnp.float32)
        diag = diag_inverse[:, index].astype(jnp.float32)
        lr, li = link[:, 0], link[:, 1]
        gr, gi = upper[:, 0], upper[:, 1]
        mr = lax.optimization_barrier((product(lr, gr) - product(li, gi)).astype(jnp.bfloat16)).astype(jnp.float32)
        mi = lax.optimization_barrier((product(lr, gi) + product(li, gr)).astype(jnp.bfloat16)).astype(jnp.float32)
        green_real = diag[:, 0] + product_t(mr, lr) - product_t(mi, li)
        green_imag = diag[:, 1] + product_t(mr, li) + product_t(mi, lr)
        term = pole_weight[:, 0][:, None, None] * green_imag + pole_weight[:, 1][:, None, None] * green_real
        return jnp.sum(term, axis=0).astype(jnp.bfloat16)

    density = lax.map(one_block, block_ids)

    def one_tile(tile):
        blocks = jnp.take(density, tile_blocks[tile], axis=0).astype(jnp.float32)
        values = orbital_values[tile].astype(jnp.float32)
        inner = jnp.einsum("spw,swv->spv", values, blocks, precision=lax.Precision.HIGHEST)
        contribution = jnp.sum(values * inner, axis=-1)
        live = (jnp.arange(SLOTS, dtype=jnp.int32) < tile_count[tile])[:, None]
        return jnp.sum(jnp.where(live, contribution, jnp.float32(0.0)), axis=0)

    return lax.map(one_tile, jnp.arange(NTILES, dtype=jnp.int32))
```

```python
import jax
import jax.numpy as jnp
from jax import lax
from jax.experimental import pallas as pl
from jax.experimental.pallas import tpu as pltpu
from jax.sharding import Mesh, PartitionSpec as P

LEVELS = 4
HALF = 128
F32 = jnp.float32
BF16 = jnp.bfloat16
SMEM = pl.BlockSpec(memory_space=pltpu.SMEM)
VMEM = pl.BlockSpec(memory_space=pltpu.VMEM)


def iotas():
    row = lax.broadcasted_iota(jnp.int32, (HALF, HALF), 0)
    col = lax.broadcasted_iota(jnp.int32, (HALF, HALF), 1)
    return row, col


def packed(t):
    row, col = iotas()
    t00, t01 = t[:HALF, :HALF], t[:HALF, HALF:]
    t10, t11 = t[HALF:, :HALF], t[HALF:, HALF:]
    here = jnp.where(col >= row, t00, t11)
    there = jnp.where(col > row, t11, jnp.where(col < row, t00, 0.0))
    diagonal = jnp.sum(jnp.where(col == row, t11, 0.0), axis=0, keepdims=True)
    return here + there.T, t01 + t10.T, diagonal


def weigh_kernel(nblocks, weight, diag, tiles, rows):
    for b in range(nblocks):
        t = weight[0, 0] * diag[b, 1].astype(F32) + weight[0, 1] * diag[b, 0].astype(F32)
        first, second, diagonal = packed(t)
        tiles[b, 0] = first
        tiles[b, 1] = second
        rows[pl.ds(b, 1), :] = diagonal


def dot(left, right):
    return lax.dot_general(left, right, (((1,), (0,)), ((), ())), preferred_element_type=F32)


def dot_t(left, right):
    return lax.dot_general(left, right, (((1,), (1,)), ((), ())), preferred_element_type=F32)


def term_kernel(nblocks, bit, core, weight, link, up0, up1, up2, up3, tiles, rows, keep, send, pair):
    for level, up in enumerate((up0, up1, up2, up3)):
        pair[level, 0, :, :256] = up[0]
        pair[level, 0, :, 256:] = up[1]
        pair[level, 1, :, :256] = -up[1]
        pair[level, 1, :, 256:] = up[0]
    first_core = core[0] == 0

    def one(b, carry):
        level = bit[b]
        lr, li = link[b, 0], link[b, 1]
        middle = (dot(lr, pair[level, 0]) + dot(li, pair[level, 1])).astype(BF16)
        mr, mi = middle[:, :256], middle[:, 256:]
        real = dot_t(mr, lr) - dot_t(mi, li)
        imag = dot_t(mr, li) + dot_t(mi, lr)
        first, second, diagonal = packed(weight[0, 0] * imag + weight[0, 1] * real)
        first = first + tiles[b, 0]
        second = second + tiles[b, 1]
        at = pl.ds(pl.multiple_of(b * HALF, HALF), HALF)
        keep[at, :] = jnp.where(first_core, first, second)
        send[at, :] = jnp.where(first_core, second, first)
        own = pl.ds(nblocks * HALF + b, 1)
        keep[own, :] = diagonal + rows[pl.ds(b, 1), :]
        return carry

    lax.fori_loop(0, nblocks, one, 0)
    tail = pl.ds(nblocks * HALF, nblocks)
    send[tail, :] = keep[tail, :]
    rest = pl.ds(nblocks * HALF + nblocks, 8)
    keep[rest, :] = jnp.zeros((8, HALF), F32)
    send[rest, :] = jnp.zeros((8, HALF), F32)


def pick_kernel(nblocks, slots, where, before, own, after, out):
    position = lax.broadcasted_iota(jnp.int32, (16, HALF), 0)
    tail = pl.ds(nblocks * HALF, 16)
    diagonals = jnp.zeros((16, HALF), F32)
    for s in range(slots):
        side, b = where[s] // nblocks, where[s] % nblocks
        at = pl.ds(pl.multiple_of(b * HALF, HALF), HALF)
        for k, source in enumerate((before, own, after)):

            @pl.when(side == k)
            def _():
                tile = source[at, :]
                for y in range(out.shape[0]):
                    out[y, pl.ds(s * HALF, HALF), :] = tile

        edge = jnp.where(side == 0, before[tail, :], jnp.where(side == 1, own[tail, :], after[tail, :]))
        line = jnp.sum(jnp.where(position == b, edge.astype(F32), 0.0), axis=0, keepdims=True)
        diagonals = jnp.where(position == s, line, diagonals)
    for y in range(out.shape[0]):
        out[y, pl.ds(slots * HALF, 16), :] = diagonals.astype(BF16)


def grid_kernel(slots, core, count, own, other, values, out):
    row, col = iotas()
    first_core = core[0] == 0
    total = jnp.zeros(values.shape[1:], F32)
    for s in range(slots):
        at = pl.ds(s * HALF, HALF)
        mine, theirs = own[at, :], other[at, :]
        first = jnp.where(first_core, mine, theirs)
        second = jnp.where(first_core, theirs, mine)
        line = own[pl.ds(slots * HALF + s, 1), :]
        upper = jnp.where(col >= row, first, 0.0)
        lower = jnp.where(col < row, first, jnp.where(col == row, line, 0.0))
        top = jnp.concatenate([upper, second], axis=1)
        bottom = jnp.concatenate([jnp.zeros_like(lower), lower], axis=1)
        block = jnp.concatenate([top, bottom], axis=0).astype(BF16)
        v = values[s]
        inner = dot(v, block)
        total = total + jnp.where(s < count[0], v.astype(F32) * inner, 0.0)
    narrow = total[:, :HALF] + total[:, HALF:]
    for k in range(narrow.shape[0] // HALF):
        piece = narrow[k * HALF : (k + 1) * HALF].T
        out[:, k * HALF : (k + 1) * HALF] = jnp.sum(piece, axis=0, keepdims=True)


def call(kernel, out_shape, in_specs, scratch=(), flops=0, moved=0):
    out_specs = jax.tree.map(lambda _: VMEM, out_shape)
    return pl.pallas_call(
        kernel,
        out_shape=out_shape,
        in_specs=in_specs,
        out_specs=out_specs,
        scratch_shapes=list(scratch),
        cost_estimate=pl.CostEstimate(flops=flops, bytes_accessed=moved, transcendentals=0),
    )


def shape(dims, dtype):
    return jax.ShapeDtypeStruct(dims, dtype)


def shards(
    diag_inverse,
    coupling,
    ancestor_inverse,
    pole_weight,
    ancestor_bit,
    tile_blocks,
    tile_count,
    orbital_values,
):
    diag, link, own_upper = diag_inverse[0], coupling[0], ancestor_inverse[0, 0]
    nblocks, slots = diag.shape[0], orbital_values.shape[1]
    nsep, groups = lax.axis_size("sep"), lax.axis_size("yh")
    core = lax.axis_index("core").astype(jnp.int32).reshape(1)
    swap = [(0, 1), (1, 0)]

    uppers = [lax.ppermute(own_upper, "sep", [(i, i ^ 1 << k) for i in range(nsep)]) for k in range(LEVELS)]
    tiles, rows = call(
        lambda *refs: weigh_kernel(nblocks, *refs),
        (shape((nblocks, 2, HALF, HALF), F32), shape((nblocks, HALF), F32)),
        [SMEM, VMEM],
        flops=2_000_000,
        moved=3_200_000,
    )(pole_weight, diag)

    length = nblocks * HALF + 16
    keep, send = call(
        lambda *refs: term_kernel(nblocks, *refs),
        (shape((length, HALF), F32), shape((length, HALF), F32)),
        [SMEM, SMEM, SMEM] + [VMEM] * 7,
        [pltpu.VMEM((LEVELS, 2, 256, 512), BF16)],
        flops=2_100_000_000,
        moved=5_000_000,
    )(ancestor_bit, core, pole_weight, link, *uppers, tiles, rows)
    chip = (keep + lax.ppermute(send, "core", swap)).astype(BF16)

    before = lax.ppermute(chip, "sep", [(i, i + 1) for i in range(nsep - 1)])
    after = lax.ppermute(chip, "sep", [(i + 1, i) for i in range(nsep - 1)])
    where = tile_blocks[0] - (lax.axis_index("sep") - 1) * nblocks
    picked = call(
        lambda *refs: pick_kernel(nblocks, slots, *refs),
        shape((groups, slots * HALF + 16, HALF), BF16),
        [SMEM] + [VMEM] * 3,
        moved=1_500_000,
    )(where, before, chip, after)
    parts = lax.all_to_all(picked, "yh", 0, 0, tiled=True)
    own = jnp.sum(parts.astype(F32), axis=0)
    other = lax.ppermute(own, "core", swap)
    return call(
        lambda *refs: grid_kernel(slots, *refs),
        shape((1, orbital_values.shape[2]), F32),
        [SMEM, SMEM] + [VMEM] * 3,
        flops=200_000_000,
        moved=1_600_000,
    )(core, tile_count, own, other, orbital_values[0])


def solution(mesh):
    pole, sep = mesh.shape["pole"], mesh.shape["sep"]
    split = Mesh(mesh.devices.reshape(pole // 2, 2, sep), ("yh", "core", "sep"))
    poles = ("yh", "core")
    placed = (
        P(poles, "sep", None, None, None),
        P(poles, "sep", None, None, None),
        P(poles, "sep", None, None, None),
        P(poles, None),
        P("sep"),
        P("sep", None),
        P("sep"),
        P("sep", None, poles, None),
    )
    return jax.shard_map(shards, mesh=split, in_specs=placed, out_specs=P("sep", poles), check_vma=False)
```

```python
import jax
import jax.numpy as jnp
from jax import lax
from jax.experimental import pallas as pl
from jax.experimental.pallas import tpu as pltpu
from jax.sharding import Mesh, PartitionSpec as P

LEVELS = 4
HALF = 128
UNROLL = 2
F32 = jnp.float32
BF16 = jnp.bfloat16
SMEM = pl.BlockSpec(memory_space=pltpu.SMEM)
VMEM = pl.BlockSpec(memory_space=pltpu.VMEM)


def iotas():
    row = lax.broadcasted_iota(jnp.int32, (HALF, HALF), 0)
    col = lax.broadcasted_iota(jnp.int32, (HALF, HALF), 1)
    return row, col


def packed(t):
    row, col = iotas()
    t00, t01 = t[:HALF, :HALF], t[:HALF, HALF:]
    t10, t11 = t[HALF:, :HALF], t[HALF:, HALF:]
    here = jnp.where(col >= row, t00, t11)
    there = jnp.where(col > row, t11, jnp.where(col < row, t00, 0.0))
    diagonal = jnp.sum(jnp.where(col == row, t11, 0.0), axis=0, keepdims=True)
    return here + there.T, t01 + t10.T, diagonal


def weigh_kernel(nblocks, weight, diag, tiles, rows):
    for b in range(nblocks):
        t = weight[0, 0] * diag[b, 1].astype(F32) + weight[0, 1] * diag[b, 0].astype(F32)
        first, second, diagonal = packed(t)
        tiles[b, 0] = first
        tiles[b, 1] = second
        rows[pl.ds(b, 1), :] = diagonal


def dot(left, right):
    return lax.dot_general(left, right, (((1,), (0,)), ((), ())), preferred_element_type=F32)


def dot_t(left, right):
    return lax.dot_general(left, right, (((1,), (1,)), ((), ())), preferred_element_type=F32)


def term_kernel(nblocks, bit, core, weight, link, up0, up1, up2, up3, tiles, rows, keep, send, pair):
    for level, up in enumerate((up0, up1, up2, up3)):
        pair[level, 0, :, :256] = up[0]
        pair[level, 0, :, 256:] = up[1]
        pair[level, 1, :, :256] = -up[1]
        pair[level, 1, :, 256:] = up[0]
    first_core = core[0] == 0
    groups = keep.shape[0]
    step = HALF // groups

    def one(b, carry):
        level = bit[b]
        lr, li = link[b, 0], link[b, 1]
        middle = (dot(lr, pair[level, 0]) + dot(li, pair[level, 1])).astype(BF16)
        mr, mi = middle[:, :256], middle[:, 256:]
        real = dot_t(mr, lr) - dot_t(mi, li)
        imag = dot_t(mr, li) + dot_t(mi, lr)
        first, second, diagonal = packed(weight[0, 0] * imag + weight[0, 1] * real)
        first = first + tiles[b, 0]
        second = second + tiles[b, 1]
        mine = jnp.where(first_core, first, second)
        theirs = jnp.where(first_core, second, first)
        at = pl.ds(pl.multiple_of(b * step, step), step)
        for y in range(groups):
            keep[y, at, :] = mine[y * step : (y + 1) * step]
            send[y, at, :] = theirs[y * step : (y + 1) * step]
        keep[0, pl.ds(nblocks * step + b, 1), :] = diagonal + rows[pl.ds(b, 1), :]
        return carry

    lax.fori_loop(0, nblocks, one, 0, unroll=UNROLL)
    tail = keep[0, pl.ds(nblocks * step, nblocks), :]
    for y in range(groups):
        for ref in (keep, send):
            ref[y, pl.ds(nblocks * step, nblocks), :] = tail
            ref[y, pl.ds(nblocks * (step + 1), 8), :] = jnp.zeros((8, HALF), F32)


def pick_kernel(nblocks, slots, where, before, own, after, out):
    groups = out.shape[0]
    step = HALF // groups
    position = lax.broadcasted_iota(jnp.int32, (16, HALF), 0)
    tail = pl.ds(nblocks * step, 16)
    diagonals = jnp.zeros((16, HALF), F32)
    for s in range(slots):
        side, b = where[s] // nblocks, where[s] % nblocks
        at = pl.ds(pl.multiple_of(b * step, step), step)
        for k, source in enumerate((before, own, after)):

            @pl.when(side == k)
            def _():
                tile = source[at, :]
                for y in range(groups):
                    out[y, pl.ds(s * step, step), :] = tile

        edge = jnp.where(side == 0, before[tail, :], jnp.where(side == 1, own[tail, :], after[tail, :]))
        line = jnp.sum(jnp.where(position == b, edge.astype(F32), 0.0), axis=0, keepdims=True)
        diagonals = jnp.where(position == s, line, diagonals)
    for y in range(groups):
        out[y, pl.ds(slots * step, 16), :] = diagonals.astype(BF16)


def grid_kernel(slots, core, count, own, other, values, out):
    row, col = iotas()
    first_core = core[0] == 0
    groups = own.shape[0]
    step = HALF // groups
    total = jnp.zeros(values.shape[1:], F32)
    lines = own[0, pl.ds(slots * step, 16), :].astype(F32)
    for s in range(slots):
        at = pl.ds(s * step, step)
        mine = jnp.concatenate([own[y, at, :] for y in range(groups)], axis=0).astype(F32)
        theirs = jnp.concatenate([other[y, at, :] for y in range(groups)], axis=0).astype(F32)
        first = jnp.where(first_core, mine, theirs)
        second = jnp.where(first_core, theirs, mine)
        upper = jnp.where(col >= row, first, 0.0)
        lower = jnp.where(col < row, first, jnp.where(col == row, lines[s : s + 1], 0.0))
        top = jnp.concatenate([upper, second], axis=1)
        bottom = jnp.concatenate([jnp.zeros_like(lower), lower], axis=1)
        block = jnp.concatenate([top, bottom], axis=0).astype(BF16)
        v = values[s]
        inner = dot(v, block)
        total = total + jnp.where(s < count[0], v.astype(F32) * inner, 0.0)
    narrow = total[:, :HALF] + total[:, HALF:]
    for k in range(narrow.shape[0] // HALF):
        piece = narrow[k * HALF : (k + 1) * HALF].T
        out[:, k * HALF : (k + 1) * HALF] = jnp.sum(piece, axis=0, keepdims=True)


def call(kernel, out_shape, in_specs, scratch=(), flops=0, moved=0, vmem=8):
    out_specs = jax.tree.map(lambda _: VMEM, out_shape)
    return pl.pallas_call(
        kernel,
        out_shape=out_shape,
        in_specs=in_specs,
        out_specs=out_specs,
        scratch_shapes=list(scratch),
        compiler_params=pltpu.CompilerParams(vmem_limit_bytes=vmem << 20),
        cost_estimate=pl.CostEstimate(flops=flops, bytes_accessed=moved, transcendentals=0),
    )


def shape(dims, dtype):
    return jax.ShapeDtypeStruct(dims, dtype)


def shards(
    diag_inverse,
    coupling,
    ancestor_inverse,
    pole_weight,
    ancestor_bit,
    tile_blocks,
    tile_count,
    orbital_values,
):
    diag, link, own_upper = diag_inverse[0], coupling[0], ancestor_inverse[0, 0]
    nblocks, slots = diag.shape[0], orbital_values.shape[1]
    nsep, groups = lax.axis_size("sep"), lax.axis_size("yh")
    core = lax.axis_index("core").astype(jnp.int32).reshape(1)
    swap = [(0, 1), (1, 0)]

    uppers = [lax.ppermute(own_upper, "sep", [(i, i ^ 1 << k) for i in range(nsep)]) for k in range(LEVELS)]
    tiles, rows = call(
        lambda *refs: weigh_kernel(nblocks, *refs),
        (shape((nblocks, 2, HALF, HALF), F32), shape((nblocks, HALF), F32)),
        [SMEM, VMEM],
        flops=2_000_000,
        moved=3_200_000,
    )(pole_weight, diag)

    step = HALF // groups
    length = nblocks * step + 16
    keep, send = call(
        lambda *refs: term_kernel(nblocks, *refs),
        (shape((groups, length, HALF), F32), shape((groups, length, HALF), F32)),
        [SMEM, SMEM, SMEM] + [VMEM] * 7,
        [pltpu.VMEM((LEVELS, 2, 256, 512), BF16)],
        flops=2_100_000_000,
        moved=5_000_000,
        vmem=16,
    )(ancestor_bit, core, pole_weight, link, *uppers, tiles, rows)
    chip = (keep + lax.ppermute(send, "core", swap)).astype(BF16)
    parts = lax.all_to_all(chip, "yh", 0, 0, tiled=True)
    held = jnp.sum(parts.astype(F32), axis=0).astype(BF16)

    before = lax.ppermute(held, "sep", [(i, i + 1) for i in range(nsep - 1)])
    after = lax.ppermute(held, "sep", [(i + 1, i) for i in range(nsep - 1)])
    where = tile_blocks[0] - (lax.axis_index("sep") - 1) * nblocks
    picked = call(
        lambda *refs: pick_kernel(nblocks, slots, *refs),
        shape((groups, slots * step + 16, HALF), BF16),
        [SMEM] + [VMEM] * 3,
        moved=500_000,
    )(where, before, held, after)
    own = lax.all_to_all(picked, "yh", 0, 0, tiled=True)
    other = lax.ppermute(own, "core", swap)
    return call(
        lambda *refs: grid_kernel(slots, *refs),
        shape((1, orbital_values.shape[2]), F32),
        [SMEM, SMEM] + [VMEM] * 3,
        flops=200_000_000,
        moved=1_300_000,
    )(core, tile_count, own, other, orbital_values[0])


def solution(mesh):
    pole, sep = mesh.shape["pole"], mesh.shape["sep"]
    split = Mesh(mesh.devices.reshape(pole // 2, 2, sep), ("yh", "core", "sep"))
    poles = ("yh", "core")
    placed = (
        P(poles, "sep", None, None, None),
        P(poles, "sep", None, None, None),
        P(poles, "sep", None, None, None),
        P(poles, None),
        P("sep"),
        P("sep", None),
        P("sep"),
        P("sep", None, poles, None),
    )
    return jax.shard_map(shards, mesh=split, in_specs=placed, out_specs=P("sep", poles), check_vma=False)
```

```python
import jax
import jax.numpy as jnp
from jax import lax
from jax.experimental import pallas as pl
from jax.experimental.pallas import tpu as pltpu
from jax.sharding import Mesh, PartitionSpec as P

LEVELS = 4
HALF = 128
F32 = jnp.float32
BF16 = jnp.bfloat16
SMEM = pl.BlockSpec(memory_space=pltpu.SMEM)
VMEM = pl.BlockSpec(memory_space=pltpu.VMEM)


def iotas():
    row = lax.broadcasted_iota(jnp.int32, (HALF, HALF), 0)
    col = lax.broadcasted_iota(jnp.int32, (HALF, HALF), 1)
    return row, col


def packed(t):
    row, col = iotas()
    t00, t01 = t[:HALF, :HALF], t[:HALF, HALF:]
    t10, t11 = t[HALF:, :HALF], t[HALF:, HALF:]
    here = jnp.where(col >= row, t00, t11)
    there = jnp.where(col > row, t11, jnp.where(col < row, t00, 0.0))
    diagonal = jnp.sum(jnp.where(col == row, t11, 0.0), axis=0, keepdims=True)
    return here + there.T, t01 + t10.T, diagonal


def weigh_kernel(nblocks, slots, weight, place, listed, count, diag, tiles, rows, plan):
    for s in range(slots):
        plan[s] = listed[0, s] - (place[0] - 1) * nblocks
    plan[slots] = count[0]
    plan[slots + 1] = place[1]
    for b in range(nblocks):
        t = weight[0, 0] * diag[b, 1].astype(F32) + weight[0, 1] * diag[b, 0].astype(F32)
        first, second, diagonal = packed(t)
        tiles[b, 0] = first
        tiles[b, 1] = second
        rows[pl.ds(b, 1), :] = diagonal


def dot(left, right):
    return lax.dot_general(left, right, (((1,), (0,)), ((), ())), preferred_element_type=F32)


def dot_t(left, right):
    return lax.dot_general(left, right, (((1,), (1,)), ((), ())), preferred_element_type=F32)


def term_kernel(nblocks, order, bit, core, weight, link, tiles, rows, *refs):
    uppers, (keep, send, pair) = refs[: len(order)], refs[len(order) :]
    for level, up in zip(order, uppers):
        pair[level, 0, :, :256] = up[0]
        pair[level, 0, :, 256:] = up[1]
        pair[level, 1, :, :256] = -up[1]
        pair[level, 1, :, 256:] = up[0]
    first_core = core[core.shape[0] - 1] == 0
    groups = keep.shape[0]
    step = HALF // groups

    def one(b):
        level = bit[b]
        lr, li = link[b, 0], link[b, 1]
        middle = (dot(lr, pair[level, 0]) + dot(li, pair[level, 1])).astype(BF16)
        mr, mi = middle[:, :256], middle[:, 256:]
        real = dot_t(mr, lr) - dot_t(mi, li)
        imag = dot_t(mr, li) + dot_t(mi, lr)
        first, second, diagonal = packed(weight[0, 0] * imag + weight[0, 1] * real)
        first = first + tiles[b, 0]
        second = second + tiles[b, 1]
        mine = jnp.where(first_core, first, second)
        theirs = jnp.where(first_core, second, first)
        at = pl.ds(b * step, step)
        for y in range(groups):
            keep[y, at, :] = mine[y * step : (y + 1) * step]
            send[y, at, :] = theirs[y * step : (y + 1) * step]
        keep[0, pl.ds(nblocks * step + b, 1), :] = diagonal + rows[pl.ds(b, 1), :]

    for b in range(nblocks):
        one(b)
    tail = keep[0, pl.ds(nblocks * step, nblocks), :]
    for y in range(groups):
        for ref in (keep, send):
            ref[y, pl.ds(nblocks * step, nblocks), :] = tail
            ref[y, pl.ds(nblocks * (step + 1), 8), :] = jnp.zeros((8, HALF), F32)


def chip_kernel(mine, theirs, out):
    out[...] = (mine[...] + theirs[...]).astype(BF16)


def group_kernel(parts, out):
    total = parts[0].astype(F32)
    for y in range(1, parts.shape[0]):
        total = total + parts[y].astype(F32)
    out[...] = total.astype(BF16)


def pick_kernel(nblocks, slots, where, before, own, after, out):
    groups = out.shape[0]
    step = HALF // groups
    position = lax.broadcasted_iota(jnp.int32, (16, HALF), 0)
    tail = pl.ds(nblocks * step, 16)
    diagonals = jnp.zeros((16, HALF), F32)
    for s in range(slots):
        side, b = where[s] // nblocks, where[s] % nblocks
        at = pl.ds(pl.multiple_of(b * step, step), step)
        for k, source in enumerate((before, own, after)):

            @pl.when(side == k)
            def _():
                tile = source[at, :]
                for y in range(groups):
                    out[y, pl.ds(s * step, step), :] = tile

        edge = jnp.where(side == 0, before[tail, :], jnp.where(side == 1, own[tail, :], after[tail, :]))
        line = jnp.sum(jnp.where(position == b, edge.astype(F32), 0.0), axis=0, keepdims=True)
        diagonals = jnp.where(position == s, line, diagonals)
    for y in range(groups):
        out[y, pl.ds(slots * step, 16), :] = diagonals.astype(BF16)


def grid_kernel(slots, plan, own, other, values, out):
    row, col = iotas()
    first_core = plan[slots + 1] == 0
    groups = own.shape[0]
    step = HALF // groups
    total = jnp.zeros(values.shape[1:], F32)
    lines = own[0, pl.ds(slots * step, 16), :].astype(F32)
    for s in range(slots):
        at = pl.ds(s * step, step)
        mine = jnp.concatenate([own[y, at, :] for y in range(groups)], axis=0).astype(F32)
        theirs = jnp.concatenate([other[y, at, :] for y in range(groups)], axis=0).astype(F32)
        first = jnp.where(first_core, mine, theirs)
        second = jnp.where(first_core, theirs, mine)
        upper = jnp.where(col >= row, first, 0.0)
        lower = jnp.where(col < row, first, jnp.where(col == row, lines[s : s + 1], 0.0))
        top = jnp.concatenate([upper, second], axis=1)
        bottom = jnp.concatenate([jnp.zeros_like(lower), lower], axis=1)
        block = jnp.concatenate([top, bottom], axis=0).astype(BF16)
        v = values[s]
        inner = dot(v, block)
        total = total + jnp.where(s < plan[slots], v.astype(F32) * inner, 0.0)
    narrow = total[:, :HALF] + total[:, HALF:]
    for k in range(narrow.shape[0] // HALF):
        piece = narrow[k * HALF : (k + 1) * HALF].T
        out[:, k * HALF : (k + 1) * HALF] = jnp.sum(piece, axis=0, keepdims=True)


def call(kernel, out_shape, in_specs, scratch=(), flops=0, moved=0, vmem=8):
    out_specs = jax.tree.map(lambda each: SMEM if each.dtype == jnp.int32 else VMEM, out_shape)
    return pl.pallas_call(
        kernel,
        out_shape=out_shape,
        in_specs=in_specs,
        out_specs=out_specs,
        scratch_shapes=list(scratch),
        compiler_params=pltpu.CompilerParams(vmem_limit_bytes=vmem << 20),
        cost_estimate=pl.CostEstimate(flops=flops, bytes_accessed=moved, transcendentals=0),
    )


def shape(dims, dtype):
    return jax.ShapeDtypeStruct(dims, dtype)


def shards(
    diag_inverse,
    coupling,
    ancestor_inverse,
    pole_weight,
    ancestor_bit,
    tile_blocks,
    tile_count,
    orbital_values,
):
    diag, link, own_upper = diag_inverse[0], coupling[0], ancestor_inverse[0, 0]
    nblocks, slots = diag.shape[0], orbital_values.shape[1]
    nsep, groups = lax.axis_size("sep"), lax.axis_size("yh")
    core = lax.axis_index("core").astype(jnp.int32)
    place = jnp.stack([lax.axis_index("sep").astype(jnp.int32), core])
    swap = [(0, 1), (1, 0)]

    order = (0, 2, 1, 3)
    uppers = [lax.ppermute(own_upper, "sep", [(i, i ^ 1 << k) for i in range(nsep)]) for k in order]
    tiles, rows, plan = call(
        lambda *refs: weigh_kernel(nblocks, slots, *refs),
        (
            shape((nblocks, 2, HALF, HALF), F32),
            shape((nblocks, HALF), F32),
            shape((slots + 2,), jnp.int32),
        ),
        [SMEM] * 4 + [VMEM],
        flops=2_000_000,
        moved=3_200_000,
    )(pole_weight, place, tile_blocks, tile_count, diag)

    step = HALF // groups
    length = nblocks * step + 16
    keep, send = call(
        lambda *refs: term_kernel(nblocks, order, *refs),
        (shape((groups, length, HALF), F32), shape((groups, length, HALF), F32)),
        [SMEM, SMEM, SMEM] + [VMEM] * 7,
        [pltpu.VMEM((LEVELS, 2, 256, 512), BF16)],
        flops=2_100_000_000,
        moved=5_000_000,
        vmem=16,
    )(ancestor_bit, plan, pole_weight, link, tiles, rows, *uppers)
    received = lax.ppermute(send, "core", swap)
    chip = call(chip_kernel, shape((groups, length, HALF), BF16), [VMEM] * 2, moved=1_400_000)(keep, received)
    parts = lax.all_to_all(chip, "yh", 0, 0, tiled=True)
    held = call(group_kernel, shape((length, HALF), BF16), [VMEM], moved=350_000)(parts)

    before = lax.ppermute(held, "sep", [(i, i + 1) for i in range(nsep - 1)])
    after = lax.ppermute(held, "sep", [(i + 1, i) for i in range(nsep - 1)])
    picked = call(
        lambda *refs: pick_kernel(nblocks, slots, *refs),
        shape((groups, slots * step + 16, HALF), BF16),
        [SMEM] + [VMEM] * 3,
        moved=500_000,
    )(plan, before, held, after)
    own = lax.all_to_all(picked, "yh", 0, 0, tiled=True)
    other = lax.ppermute(own, "core", swap)
    return call(
        lambda *refs: grid_kernel(slots, *refs),
        shape((1, orbital_values.shape[2]), F32),
        [SMEM] + [VMEM] * 3,
        flops=200_000_000,
        moved=1_300_000,
    )(plan, own, other, orbital_values[0])


def solution(mesh):
    pole, sep = mesh.shape["pole"], mesh.shape["sep"]
    split = Mesh(mesh.devices.reshape(pole // 2, 2, sep), ("yh", "core", "sep"))
    poles = ("yh", "core")
    placed = (
        P(poles, "sep", None, None, None),
        P(poles, "sep", None, None, None),
        P(poles, "sep", None, None, None),
        P(poles, None),
        P("sep"),
        P("sep", None),
        P("sep"),
        P("sep", None, poles, None),
    )
    return jax.shard_map(shards, mesh=split, in_specs=placed, out_specs=P("sep", poles), check_vma=False)
```

```python
import jax
import jax.numpy as jnp
from jax import lax
from jax.experimental import pallas as pl
from jax.experimental.pallas import tpu as pltpu
from jax.sharding import Mesh, PartitionSpec as P

LEVELS = 4
HALF = 128
F32 = jnp.float32
BF16 = jnp.bfloat16
SMEM = pl.BlockSpec(memory_space=pltpu.SMEM)
VMEM = pl.BlockSpec(memory_space=pltpu.VMEM)


def iotas():
    row = lax.broadcasted_iota(jnp.int32, (HALF, HALF), 0)
    col = lax.broadcasted_iota(jnp.int32, (HALF, HALF), 1)
    return row, col


def packed(t):
    row, col = iotas()
    t00, t01 = t[:HALF, :HALF], t[:HALF, HALF:]
    t10, t11 = t[HALF:, :HALF], t[HALF:, HALF:]
    here = jnp.where(col >= row, t00, t11)
    there = jnp.where(col > row, t11, jnp.where(col < row, t00, 0.0))
    diagonal = jnp.sum(jnp.where(col == row, t11, 0.0), axis=0, keepdims=True)
    return here + there.T, t01 + t10.T, diagonal


def weigh_kernel(nblocks, weight, diag, tiles, rows):
    for b in range(nblocks):
        t = weight[0, 0] * diag[b, 1].astype(F32) + weight[0, 1] * diag[b, 0].astype(F32)
        first, second, diagonal = packed(t)
        tiles[b, 0] = first
        tiles[b, 1] = second
        rows[pl.ds(b, 1), :] = diagonal


def dot(left, right):
    return lax.dot_general(left, right, (((1,), (0,)), ((), ())), preferred_element_type=F32)


def dot_t(left, right):
    return lax.dot_general(left, right, (((1,), (1,)), ((), ())), preferred_element_type=F32)


def term_kernel(nblocks, order, bit, weight, link, tiles, rows, *refs):
    uppers, (keep, send, pair) = refs[: len(order)], refs[len(order) :]
    for level, up in zip(order, uppers):
        pair[level, 0, :, :256] = up[0]
        pair[level, 0, :, 256:] = up[1]
        pair[level, 1, :, :256] = -up[1]
        pair[level, 1, :, 256:] = up[0]
    first_core = lax.axis_index("core") == 0
    for b in range(nblocks):
        level = bit[b]
        lr, li = link[b, 0], link[b, 1]
        middle = (dot(lr, pair[level, 0]) + dot(li, pair[level, 1])).astype(BF16)
        mr, mi = middle[:, :256], middle[:, 256:]
        real = dot_t(mr, lr) - dot_t(mi, li)
        imag = dot_t(mr, li) + dot_t(mi, lr)
        first, second, diagonal = packed(weight[0, 0] * imag + weight[0, 1] * real)
        first = first + tiles[b, 0]
        second = second + tiles[b, 1]
        at = pl.ds(b * HALF, HALF)
        keep[at, :] = jnp.where(first_core, first, second)
        send[at, :] = jnp.where(first_core, second, first)
        keep[pl.ds(nblocks * HALF + b, 1), :] = diagonal + rows[pl.ds(b, 1), :]
    tail = pl.ds(nblocks * HALF, nblocks)
    send[tail, :] = keep[tail, :]
    rest = pl.ds(nblocks * (HALF + 1), 8)
    keep[rest, :] = jnp.zeros((8, HALF), F32)
    send[rest, :] = jnp.zeros((8, HALF), F32)


def chip_kernel(mine, theirs, out):
    out[...] = (mine[...] + theirs[...]).astype(BF16)


def pick_kernel(nblocks, slots, listed, before, own, after, out):
    groups = out.shape[0]
    base = (lax.axis_index("sep") - 1) * nblocks
    position = lax.broadcasted_iota(jnp.int32, (16, HALF), 0)
    tail = pl.ds(nblocks * HALF, 16)
    edges = [each[tail, :].astype(F32) for each in (before, own, after)]
    diagonals = jnp.zeros((16, HALF), F32)
    for s in range(slots):
        where = listed[0, s] - base
        side, b = where // nblocks, where % nblocks
        at = pl.ds(pl.multiple_of(b * HALF, HALF), HALF)
        for k, source in enumerate((before, own, after)):

            @pl.when(side == k)
            def _():
                tile = source[at, :]
                for y in range(groups):
                    out[y, pl.ds(s * HALF, HALF), :] = tile

        edge = jnp.where(side == 0, edges[0], jnp.where(side == 1, edges[1], edges[2]))
        line = jnp.sum(jnp.where(position == b, edge, 0.0), axis=0, keepdims=True)
        diagonals = jnp.where(position == s, line, diagonals)
    for y in range(groups):
        out[y, pl.ds(slots * HALF, 16), :] = diagonals.astype(BF16)


def group_kernel(parts, out):
    total = parts[0].astype(F32)
    for y in range(1, parts.shape[0]):
        total = total + parts[y].astype(F32)
    out[...] = total.astype(BF16)


def grid_kernel(slots, count, own, other, values, out):
    row, col = iotas()
    first_core = lax.axis_index("core") == 0
    total = jnp.zeros(values.shape[1:], F32)
    lines = own[pl.ds(slots * HALF, 16), :].astype(F32)
    for s in range(slots):
        at = pl.ds(s * HALF, HALF)
        mine, theirs = own[at, :].astype(F32), other[at, :].astype(F32)
        first = jnp.where(first_core, mine, theirs)
        second = jnp.where(first_core, theirs, mine)
        upper = jnp.where(col >= row, first, 0.0)
        lower = jnp.where(col < row, first, jnp.where(col == row, lines[s : s + 1], 0.0))
        top = jnp.concatenate([upper, second], axis=1)
        bottom = jnp.concatenate([jnp.zeros_like(lower), lower], axis=1)
        block = jnp.concatenate([top, bottom], axis=0).astype(BF16)
        v = values[s]
        inner = dot(v, block)
        total = total + jnp.where(s < count[0], v.astype(F32) * inner, 0.0)
    narrow = total[:, :HALF] + total[:, HALF:]
    for k in range(narrow.shape[0] // HALF):
        piece = narrow[k * HALF : (k + 1) * HALF].T
        out[:, k * HALF : (k + 1) * HALF] = jnp.sum(piece, axis=0, keepdims=True)


def call(kernel, out_shape, in_specs, scratch=(), flops=0, moved=0, vmem=8):
    out_specs = jax.tree.map(lambda _: VMEM, out_shape)
    return pl.pallas_call(
        kernel,
        out_shape=out_shape,
        in_specs=in_specs,
        out_specs=out_specs,
        scratch_shapes=list(scratch),
        compiler_params=pltpu.CompilerParams(vmem_limit_bytes=vmem << 20),
        cost_estimate=pl.CostEstimate(flops=flops, bytes_accessed=moved, transcendentals=0),
    )


def shape(dims, dtype):
    return jax.ShapeDtypeStruct(dims, dtype)


def shards(
    diag_inverse,
    coupling,
    ancestor_inverse,
    pole_weight,
    ancestor_bit,
    tile_blocks,
    tile_count,
    orbital_values,
):
    diag, link, own_upper = diag_inverse[0], coupling[0], ancestor_inverse[0, 0]
    nblocks, slots = diag.shape[0], orbital_values.shape[1]
    nsep, groups = lax.axis_size("sep"), lax.axis_size("yh")
    swap = [(0, 1), (1, 0)]

    order = (3, 1, 2, 0)
    uppers = [lax.ppermute(own_upper, "sep", [(i, i ^ 1 << k) for i in range(nsep)]) for k in order]
    tiles, rows = call(
        lambda *refs: weigh_kernel(nblocks, *refs),
        (shape((nblocks, 2, HALF, HALF), F32), shape((nblocks, HALF), F32)),
        [SMEM, VMEM],
        flops=2_000_000,
        moved=3_200_000,
    )(pole_weight, diag)

    length = nblocks * HALF + 16
    keep, send = call(
        lambda *refs: term_kernel(nblocks, order, *refs),
        (shape((length, HALF), F32), shape((length, HALF), F32)),
        [SMEM, SMEM] + [VMEM] * (3 + LEVELS),
        [pltpu.VMEM((LEVELS, 2, 256, 512), BF16)],
        flops=2_100_000_000,
        moved=5_000_000,
        vmem=16,
    )(ancestor_bit, pole_weight, link, tiles, rows, *uppers)
    received = lax.ppermute(send, "core", swap)
    chip = call(chip_kernel, shape((length, HALF), BF16), [VMEM] * 2, moved=1_400_000)(keep, received)

    before = lax.ppermute(chip, "sep", [(i, i + 1) for i in range(nsep - 1)])
    after = lax.ppermute(chip, "sep", [(i + 1, i) for i in range(nsep - 1)])
    span = slots * HALF + 16
    picked = call(
        lambda *refs: pick_kernel(nblocks, slots, *refs),
        shape((groups, span, HALF), BF16),
        [SMEM] + [VMEM] * 3,
        moved=1_500_000,
    )(tile_blocks, before, chip, after)
    parts = lax.all_to_all(picked, "yh", 0, 0, tiled=True)
    own = call(group_kernel, shape((span, HALF), BF16), [VMEM], moved=1_000_000)(parts)
    other = lax.ppermute(own, "core", swap)
    return call(
        lambda *refs: grid_kernel(slots, *refs),
        shape((1, orbital_values.shape[2]), F32),
        [SMEM] + [VMEM] * 3,
        flops=200_000_000,
        moved=1_300_000,
    )(tile_count, own, other, orbital_values[0])


def solution(mesh):
    pole, sep = mesh.shape["pole"], mesh.shape["sep"]
    split = Mesh(mesh.devices.reshape(pole // 2, 2, sep), ("yh", "core", "sep"))
    poles = ("yh", "core")
    placed = (
        P(poles, "sep", None, None, None),
        P(poles, "sep", None, None, None),
        P(poles, "sep", None, None, None),
        P(poles, None),
        P("sep"),
        P("sep", None),
        P("sep"),
        P("sep", None, poles, None),
    )
    return jax.shard_map(shards, mesh=split, in_specs=placed, out_specs=P("sep", poles), check_vma=False)
```

```python
import jax
import jax.numpy as jnp
from jax import lax
from jax.experimental import pallas as pl
from jax.experimental.pallas import tpu as pltpu
from jax.sharding import Mesh, PartitionSpec as P

LEVELS = 4
HALF = 128
F32 = jnp.float32
BF16 = jnp.bfloat16
SMEM = pl.BlockSpec(memory_space=pltpu.SMEM)
VMEM = pl.BlockSpec(memory_space=pltpu.VMEM)


def iotas():
    row = lax.broadcasted_iota(jnp.int32, (HALF, HALF), 0)
    col = lax.broadcasted_iota(jnp.int32, (HALF, HALF), 1)
    return row, col


def packed(t):
    row, col = iotas()
    t00, t01 = t[:HALF, :HALF], t[:HALF, HALF:]
    t10, t11 = t[HALF:, :HALF], t[HALF:, HALF:]
    here = jnp.where(col >= row, t00, t11)
    there = jnp.where(col > row, t11, jnp.where(col < row, t00, 0.0))
    diagonal = jnp.sum(jnp.where(col == row, t11, 0.0), axis=0, keepdims=True)
    return here + there.T, t01 + t10.T, diagonal


def weigh_kernel(nblocks, weight, diag, tiles, rows):
    for b in range(nblocks):
        t = weight[0, 0] * diag[b, 1].astype(F32) + weight[0, 1] * diag[b, 0].astype(F32)
        first, second, diagonal = packed(t)
        tiles[b, 0] = first
        tiles[b, 1] = second
        rows[pl.ds(b, 1), :] = diagonal


def dot(left, right):
    return lax.dot_general(left, right, (((1,), (0,)), ((), ())), preferred_element_type=F32)


def dot_t(left, right):
    return lax.dot_general(left, right, (((1,), (1,)), ((), ())), preferred_element_type=F32)


def term_kernel(nblocks, order, bit, weight, link, tiles, rows, *refs):
    uppers, (keep, send, pair) = refs[: len(order)], refs[len(order) :]
    for level, up in zip(order, uppers):
        pair[level, 0, :, :256] = up[0]
        pair[level, 0, :, 256:] = up[1]
        pair[level, 1, :, :256] = -up[1]
        pair[level, 1, :, 256:] = up[0]
    first_core = lax.axis_index("core") == 0
    for b in range(nblocks):
        level = bit[b]
        lr, li = link[b, 0], link[b, 1]
        middle = (dot(lr, pair[level, 0]) + dot(li, pair[level, 1])).astype(BF16)
        mr, mi = middle[:, :256], middle[:, 256:]
        real = dot_t(mr, lr) - dot_t(mi, li)
        imag = dot_t(mr, li) + dot_t(mi, lr)
        first, second, diagonal = packed(weight[0, 0] * imag + weight[0, 1] * real)
        first = first + tiles[b, 0]
        second = second + tiles[b, 1]
        at = pl.ds(b * HALF, HALF)
        keep[at, :] = jnp.where(first_core, first, second)
        send[at, :] = jnp.where(first_core, second, first)
        keep[pl.ds(nblocks * HALF + b, 1), :] = diagonal + rows[pl.ds(b, 1), :]
    tail = pl.ds(nblocks * HALF, nblocks)
    send[tail, :] = keep[tail, :]
    rest = pl.ds(nblocks * (HALF + 1), 8)
    keep[rest, :] = jnp.zeros((8, HALF), F32)
    send[rest, :] = jnp.zeros((8, HALF), F32)


def chip_kernel(mine, theirs, out):
    out[...] = (mine[...] + theirs[...]).astype(BF16)


def pick_kernel(nblocks, slots, listed, before, own, after, out):
    groups = out.shape[0]
    base = (lax.axis_index("sep") - 1) * nblocks
    position = lax.broadcasted_iota(jnp.int32, (16, HALF), 0)
    tail = pl.ds(nblocks * HALF, 16)
    edges = [each[tail, :].astype(F32) for each in (before, own, after)]
    diagonals = jnp.zeros((16, HALF), F32)
    for s in range(slots):
        where = listed[0, s] - base
        side, b = where // nblocks, where % nblocks
        at = pl.ds(pl.multiple_of(b * HALF, HALF), HALF)
        for k, source in enumerate((before, own, after)):

            @pl.when(side == k)
            def _():
                tile = source[at, :]
                for y in range(groups):
                    out[y, pl.ds(s * HALF, HALF), :] = tile

        edge = jnp.where(side == 0, edges[0], jnp.where(side == 1, edges[1], edges[2]))
        line = jnp.sum(jnp.where(position == b, edge, 0.0), axis=0, keepdims=True)
        diagonals = jnp.where(position == s, line, diagonals)
    for y in range(groups):
        out[y, pl.ds(slots * HALF, 16), :] = diagonals.astype(BF16)


def group_kernel(parts, out):
    total = parts[0].astype(F32)
    for y in range(1, parts.shape[0]):
        total = total + parts[y].astype(F32)
    out[...] = total.astype(BF16)


def grid_kernel(slots, count, own, other, values, out):
    row, col = iotas()
    first_core = lax.axis_index("core") == 0
    total = jnp.zeros(values.shape[1:], F32)
    lines = own[pl.ds(slots * HALF, 16), :].astype(F32)
    for s in range(slots):
        at = pl.ds(s * HALF, HALF)
        mine, theirs = own[at, :].astype(F32), other[at, :].astype(F32)
        first = jnp.where(first_core, mine, theirs)
        second = jnp.where(first_core, theirs, mine)
        upper = jnp.where(col >= row, first, 0.0)
        lower = jnp.where(col < row, first, jnp.where(col == row, lines[s : s + 1], 0.0))
        top = jnp.concatenate([upper, second], axis=1)
        bottom = jnp.concatenate([jnp.zeros_like(lower), lower], axis=1)
        block = jnp.concatenate([top, bottom], axis=0).astype(BF16)
        v = values[s]
        inner = dot(v, block)
        total = total + jnp.where(s < count[0], v.astype(F32) * inner, 0.0)
    narrow = total[:, :HALF] + total[:, HALF:]
    for k in range(narrow.shape[0] // HALF):
        piece = narrow[k * HALF : (k + 1) * HALF].T
        out[:, k * HALF : (k + 1) * HALF] = jnp.sum(piece, axis=0, keepdims=True)


def call(kernel, out_shape, in_specs, scratch=(), flops=0, moved=0, vmem=8):
    out_specs = jax.tree.map(lambda _: VMEM, out_shape)
    return pl.pallas_call(
        kernel,
        out_shape=out_shape,
        in_specs=in_specs,
        out_specs=out_specs,
        scratch_shapes=list(scratch),
        compiler_params=pltpu.CompilerParams(vmem_limit_bytes=vmem << 20),
        cost_estimate=pl.CostEstimate(flops=flops, bytes_accessed=moved, transcendentals=0),
    )


def shape(dims, dtype):
    return jax.ShapeDtypeStruct(dims, dtype)


def shards(
    diag_inverse,
    coupling,
    ancestor_inverse,
    pole_weight,
    ancestor_bit,
    tile_blocks,
    tile_count,
    orbital_values,
):
    diag, link, own_upper = diag_inverse[0], coupling[0], ancestor_inverse[0, 0]
    nblocks, slots = diag.shape[0], orbital_values.shape[1]
    nsep, groups = lax.axis_size("sep"), lax.axis_size("yh")
    swap = [(0, 1), (1, 0)]

    order = (3, 0, 2, 1)
    uppers = [lax.ppermute(own_upper, "sep", [(i, i ^ 1 << k) for i in range(nsep)]) for k in order]
    tiles, rows = call(
        lambda *refs: weigh_kernel(nblocks, *refs),
        (shape((nblocks, 2, HALF, HALF), F32), shape((nblocks, HALF), F32)),
        [SMEM, VMEM],
        flops=2_000_000,
        moved=3_200_000,
    )(pole_weight, diag)

    length = nblocks * HALF + 16
    keep, send = call(
        lambda *refs: term_kernel(nblocks, order, *refs),
        (shape((length, HALF), F32), shape((length, HALF), F32)),
        [SMEM, SMEM] + [VMEM] * (3 + LEVELS),
        [pltpu.VMEM((LEVELS, 2, 256, 512), BF16)],
        flops=2_100_000_000,
        moved=5_000_000,
        vmem=16,
    )(ancestor_bit, pole_weight, link, tiles, rows, *uppers)
    received = lax.ppermute(send, "core", swap)
    chip = call(chip_kernel, shape((length, HALF), BF16), [VMEM] * 2, moved=1_400_000)(keep, received)

    before = lax.ppermute(chip, "sep", [(i, i + 1) for i in range(nsep - 1)])
    after = lax.ppermute(chip, "sep", [(i + 1, i) for i in range(nsep - 1)])
    span = slots * HALF + 16
    picked = call(
        lambda *refs: pick_kernel(nblocks, slots, *refs),
        shape((groups, span, HALF), BF16),
        [SMEM] + [VMEM] * 3,
        moved=1_500_000,
    )(tile_blocks, before, chip, after)
    parts = lax.all_to_all(picked, "yh", 0, 0, tiled=True)
    own = call(group_kernel, shape((span, HALF), BF16), [VMEM], moved=1_000_000)(parts)
    other = lax.ppermute(own, "core", swap)
    return call(
        lambda *refs: grid_kernel(slots, *refs),
        shape((1, orbital_values.shape[2]), F32),
        [SMEM] + [VMEM] * 3,
        flops=200_000_000,
        moved=1_300_000,
    )(tile_count, own, other, orbital_values[0])


def solution(mesh):
    pole, sep = mesh.shape["pole"], mesh.shape["sep"]
    split = Mesh(mesh.devices.reshape(pole // 2, 2, sep), ("yh", "core", "sep"))
    poles = ("yh", "core")
    placed = (
        P(poles, "sep", None, None, None),
        P(poles, "sep", None, None, None),
        P(poles, "sep", None, None, None),
        P(poles, None),
        P("sep"),
        P("sep", None),
        P("sep"),
        P("sep", None, poles, None),
    )
    return jax.shard_map(shards, mesh=split, in_specs=placed, out_specs=P("sep", poles), check_vma=False)
```

```python
import jax
import jax.numpy as jnp
from jax import lax
from jax.experimental import pallas as pl
from jax.experimental.pallas import tpu as pltpu
from jax.sharding import Mesh, PartitionSpec as P

LEVELS = 4
HALF = 128
F32 = jnp.float32
BF16 = jnp.bfloat16
SMEM = pl.BlockSpec(memory_space=pltpu.SMEM)
VMEM = pl.BlockSpec(memory_space=pltpu.VMEM)


def iotas():
    row = lax.broadcasted_iota(jnp.int32, (HALF, HALF), 0)
    col = lax.broadcasted_iota(jnp.int32, (HALF, HALF), 1)
    return row, col


def packed(t):
    row, col = iotas()
    t00, t01 = t[:HALF, :HALF], t[:HALF, HALF:]
    t10, t11 = t[HALF:, :HALF], t[HALF:, HALF:]
    here = jnp.where(col >= row, t00, t11)
    there = jnp.where(col > row, t11, jnp.where(col < row, t00, 0.0))
    diagonal = jnp.sum(jnp.where(col == row, t11, 0.0), axis=0, keepdims=True)
    return here + there.T, t01 + t10.T, diagonal


def weigh_kernel(nblocks, weight, diag, tiles, rows):
    for b in range(nblocks):
        t = weight[0, 0] * diag[b, 1].astype(F32) + weight[0, 1] * diag[b, 0].astype(F32)
        first, second, diagonal = packed(t)
        tiles[b, 0] = first
        tiles[b, 1] = second
        rows[pl.ds(b, 1), :] = diagonal


def dot(left, right):
    return lax.dot_general(left, right, (((1,), (0,)), ((), ())), preferred_element_type=F32)


def dot_t(left, right):
    return lax.dot_general(left, right, (((1,), (1,)), ((), ())), preferred_element_type=F32)


def term_kernel(nblocks, order, bit, weight, link, tiles, rows, *refs):
    uppers, (keep, send, pair) = refs[: len(order)], refs[len(order) :]
    for level, up in zip(order, uppers):
        pair[level, 0, :, :256] = up[0]
        pair[level, 0, :, 256:] = up[1]
        pair[level, 1, :, :256] = -up[1]
        pair[level, 1, :, 256:] = up[0]
    first_core = lax.axis_index("core") == 0
    groups = keep.shape[0]
    step = HALF // groups
    for b in range(nblocks):
        level = bit[b]
        lr, li = link[b, 0], link[b, 1]
        middle = (dot(lr, pair[level, 0]) + dot(li, pair[level, 1])).astype(BF16)
        mr, mi = middle[:, :256], middle[:, 256:]
        real = dot_t(mr, lr) - dot_t(mi, li)
        imag = dot_t(mr, li) + dot_t(mi, lr)
        first, second, diagonal = packed(weight[0, 0] * imag + weight[0, 1] * real)
        first = first + tiles[b, 0]
        second = second + tiles[b, 1]
        mine = jnp.where(first_core, first, second)
        theirs = jnp.where(first_core, second, first)
        at = pl.ds(b * step, step)
        for y in range(groups):
            keep[y, at, :] = mine[y * step : (y + 1) * step]
            send[y, at, :] = theirs[y * step : (y + 1) * step]
        keep[0, pl.ds(nblocks * step + b, 1), :] = diagonal + rows[pl.ds(b, 1), :]
    tail = keep[0, pl.ds(nblocks * step, nblocks), :]
    for y in range(groups):
        for ref in (keep, send):
            ref[y, pl.ds(nblocks * step, nblocks), :] = tail
            ref[y, pl.ds(nblocks * (step + 1), 8), :] = jnp.zeros((8, HALF), F32)


def chip_kernel(mine, theirs, out):
    out[...] = (mine[...] + theirs[...]).astype(BF16)


def pick_kernel(nblocks, slots, listed, before, own, after, out):
    groups = out.shape[0]
    step = HALF // groups
    base = (lax.axis_index("sep") - 1) * nblocks
    position = lax.broadcasted_iota(jnp.int32, (16, HALF), 0)
    tail = pl.ds(nblocks * step, 16)
    edges = [each[tail, :].astype(F32) for each in (before, own, after)]
    diagonals = jnp.zeros((16, HALF), F32)
    for s in range(slots):
        where = listed[0, s] - base
        side, b = where // nblocks, where % nblocks
        at = pl.ds(pl.multiple_of(b * step, step), step)
        for k, source in enumerate((before, own, after)):

            @pl.when(side == k)
            def _():
                tile = source[at, :]
                for y in range(groups):
                    out[y, pl.ds(s * step, step), :] = tile

        edge = jnp.where(side == 0, edges[0], jnp.where(side == 1, edges[1], edges[2]))
        line = jnp.sum(jnp.where(position == b, edge, 0.0), axis=0, keepdims=True)
        diagonals = jnp.where(position == s, line, diagonals)
    for y in range(groups):
        out[y, pl.ds(slots * step, 16), :] = diagonals.astype(BF16)


def group_kernel(parts, out):
    total = parts[0].astype(F32)
    for y in range(1, parts.shape[0]):
        total = total + parts[y].astype(F32)
    out[...] = total.astype(BF16)


def grid_kernel(slots, count, own, other, values, out):
    row, col = iotas()
    first_core = lax.axis_index("core") == 0
    groups = own.shape[0]
    step = HALF // groups
    total = jnp.zeros(values.shape[1:], F32)
    lines = own[0, pl.ds(slots * step, 16), :].astype(F32)
    for s in range(slots):
        at = pl.ds(s * step, step)
        mine = jnp.concatenate([own[y, at, :] for y in range(groups)], axis=0).astype(F32)
        theirs = jnp.concatenate([other[y, at, :] for y in range(groups)], axis=0).astype(F32)
        first = jnp.where(first_core, mine, theirs)
        second = jnp.where(first_core, theirs, mine)
        upper = jnp.where(col >= row, first, 0.0)
        lower = jnp.where(col < row, first, jnp.where(col == row, lines[s : s + 1], 0.0))
        top = jnp.concatenate([upper, second], axis=1)
        bottom = jnp.concatenate([jnp.zeros_like(lower), lower], axis=1)
        block = jnp.concatenate([top, bottom], axis=0).astype(BF16)
        v = values[s]
        inner = dot(v, block)
        total = total + jnp.where(s < count[0], v.astype(F32) * inner, 0.0)
    narrow = total[:, :HALF] + total[:, HALF:]
    for k in range(narrow.shape[0] // HALF):
        piece = narrow[k * HALF : (k + 1) * HALF].T
        out[:, k * HALF : (k + 1) * HALF] = jnp.sum(piece, axis=0, keepdims=True)


def call(kernel, out_shape, in_specs, scratch=(), flops=0, moved=0, vmem=8):
    out_specs = jax.tree.map(lambda _: VMEM, out_shape)
    return pl.pallas_call(
        kernel,
        out_shape=out_shape,
        in_specs=in_specs,
        out_specs=out_specs,
        scratch_shapes=list(scratch),
        compiler_params=pltpu.CompilerParams(vmem_limit_bytes=vmem << 20),
        cost_estimate=pl.CostEstimate(flops=flops, bytes_accessed=moved, transcendentals=0),
    )


def shape(dims, dtype):
    return jax.ShapeDtypeStruct(dims, dtype)


def shards(
    diag_inverse,
    coupling,
    ancestor_inverse,
    pole_weight,
    ancestor_bit,
    tile_blocks,
    tile_count,
    orbital_values,
):
    diag, link, own_upper = diag_inverse[0], coupling[0], ancestor_inverse[0, 0]
    nblocks, slots = diag.shape[0], orbital_values.shape[1]
    nsep, groups = lax.axis_size("sep"), lax.axis_size("yh")
    swap = [(0, 1), (1, 0)]

    order = (2, 0, 3, 1)
    uppers = [lax.ppermute(own_upper, "sep", [(i, i ^ 1 << k) for i in range(nsep)]) for k in order]
    tiles, rows = call(
        lambda *refs: weigh_kernel(nblocks, *refs),
        (shape((nblocks, 2, HALF, HALF), F32), shape((nblocks, HALF), F32)),
        [SMEM, VMEM],
        flops=2_000_000,
        moved=3_200_000,
    )(pole_weight, diag)

    step = HALF // groups
    length = nblocks * step + 16
    keep, send = call(
        lambda *refs: term_kernel(nblocks, order, *refs),
        (shape((groups, length, HALF), F32), shape((groups, length, HALF), F32)),
        [SMEM, SMEM] + [VMEM] * (3 + LEVELS),
        [pltpu.VMEM((LEVELS, 2, 256, 512), BF16)],
        flops=2_100_000_000,
        moved=5_000_000,
        vmem=16,
    )(ancestor_bit, pole_weight, link, tiles, rows, *uppers)
    received = lax.ppermute(send, "core", swap)
    chip = call(chip_kernel, shape((groups, length, HALF), BF16), [VMEM] * 2, moved=1_400_000)(keep, received)
    parts = lax.all_to_all(chip, "yh", 0, 0, tiled=True)
    held = call(group_kernel, shape((length, HALF), BF16), [VMEM], moved=350_000)(parts)

    before = lax.ppermute(held, "sep", [(i, i + 1) for i in range(nsep - 1)])
    after = lax.ppermute(held, "sep", [(i + 1, i) for i in range(nsep - 1)])
    picked = call(
        lambda *refs: pick_kernel(nblocks, slots, *refs),
        shape((groups, slots * step + 16, HALF), BF16),
        [SMEM] + [VMEM] * 3,
        moved=500_000,
    )(tile_blocks, before, held, after)
    own = lax.all_to_all(picked, "yh", 0, 0, tiled=True)
    other = lax.ppermute(own, "core", swap)
    return call(
        lambda *refs: grid_kernel(slots, *refs),
        shape((1, orbital_values.shape[2]), F32),
        [SMEM] + [VMEM] * 3,
        flops=200_000_000,
        moved=1_300_000,
    )(tile_count, own, other, orbital_values[0])


def solution(mesh):
    pole, sep = mesh.shape["pole"], mesh.shape["sep"]
    split = Mesh(mesh.devices.reshape(pole // 2, 2, sep), ("yh", "core", "sep"))
    poles = ("yh", "core")
    placed = (
        P(poles, "sep", None, None, None),
        P(poles, "sep", None, None, None),
        P(poles, "sep", None, None, None),
        P(poles, None),
        P("sep"),
        P("sep", None),
        P("sep"),
        P("sep", None, poles, None),
    )
    return jax.shard_map(shards, mesh=split, in_specs=placed, out_specs=P("sep", poles), check_vma=False)
```

```python
import jax
import jax.numpy as jnp
from jax import lax
from jax.experimental import pallas as pl
from jax.experimental.pallas import tpu as pltpu
from jax.sharding import Mesh, PartitionSpec as P

LEVELS = 4
HALF = 128
F32 = jnp.float32
BF16 = jnp.bfloat16
SMEM = pl.BlockSpec(memory_space=pltpu.SMEM)
VMEM = pl.BlockSpec(memory_space=pltpu.VMEM)


def iotas():
    row = lax.broadcasted_iota(jnp.int32, (HALF, HALF), 0)
    col = lax.broadcasted_iota(jnp.int32, (HALF, HALF), 1)
    return row, col


def packed(t):
    row, col = iotas()
    t00, t01 = t[:HALF, :HALF], t[:HALF, HALF:]
    t10, t11 = t[HALF:, :HALF], t[HALF:, HALF:]
    here = jnp.where(col >= row, t00, t11)
    there = jnp.where(col > row, t11, jnp.where(col < row, t00, 0.0))
    diagonal = jnp.sum(jnp.where(col == row, t11, 0.0), axis=0, keepdims=True)
    return here + there.T, t01 + t10.T, diagonal


def weigh_kernel(nblocks, weight, diag, tiles, rows):
    for b in range(nblocks):
        t = weight[0, 0] * diag[b, 1].astype(F32) + weight[0, 1] * diag[b, 0].astype(F32)
        first, second, diagonal = packed(t)
        tiles[b, 0] = first
        tiles[b, 1] = second
        rows[pl.ds(b, 1), :] = diagonal


def dot(left, right):
    return lax.dot_general(left, right, (((1,), (0,)), ((), ())), preferred_element_type=F32)


def dot_t(left, right):
    return lax.dot_general(left, right, (((1,), (1,)), ((), ())), preferred_element_type=F32)


def term_kernel(nblocks, order, bit, weight, link, tiles, rows, *refs):
    uppers, (keep, send, pair) = refs[: len(order)], refs[len(order) :]
    for level, up in zip(order, uppers):
        pair[level, 0, :, :256] = up[0]
        pair[level, 0, :, 256:] = up[1]
        pair[level, 1, :, :256] = -up[1]
        pair[level, 1, :, 256:] = up[0]
    first_core = lax.axis_index("core") == 0
    groups = keep.shape[0]
    step = HALF // groups
    for b in range(nblocks):
        level = bit[b]
        lr, li = link[b, 0], link[b, 1]
        middle = (dot(lr, pair[level, 0]) + dot(li, pair[level, 1])).astype(BF16)
        mr, mi = middle[:, :256], middle[:, 256:]
        real = dot_t(mr, lr) - dot_t(mi, li)
        imag = dot_t(mr, li) + dot_t(mi, lr)
        first, second, diagonal = packed(weight[0, 0] * imag + weight[0, 1] * real)
        first = first + tiles[b, 0]
        second = second + tiles[b, 1]
        mine = jnp.where(first_core, first, second)
        theirs = jnp.where(first_core, second, first)
        at = pl.ds(b * step, step)
        for y in range(groups):
            keep[y, at, :] = mine[y * step : (y + 1) * step]
            send[y, at, :] = theirs[y * step : (y + 1) * step].astype(BF16)
        keep[0, pl.ds(nblocks * step + b, 1), :] = diagonal + rows[pl.ds(b, 1), :]
    tail = pl.ds(nblocks * step, 16)
    keep[0, pl.ds(nblocks * step + nblocks, 16 - nblocks), :] = jnp.zeros((16 - nblocks, HALF), F32)
    edge = keep[0, tail, :]
    for y in range(groups):
        keep[y, tail, :] = edge
        send[y, tail, :] = edge.astype(BF16)


def chip_kernel(mine, theirs, out):
    out[...] = (mine[...] + theirs[...].astype(F32)).astype(BF16)


def pick_kernel(nblocks, slots, listed, before, own, after, out, near):
    groups, length = out.shape[0], own.shape[0]
    step = HALF // groups
    base = (lax.axis_index("sep") - 1) * nblocks
    position = lax.broadcasted_iota(jnp.int32, (16, HALF), 0)
    for k, source in enumerate((before, own, after)):
        near[pl.ds(k * length, length), :] = source[...]
    diagonals = jnp.zeros((16, HALF), F32)
    for s in range(slots):
        where = listed[0, s] - base
        side, b = where // nblocks, where % nblocks
        tile = near[pl.ds(pl.multiple_of(side * length + b * step, 16), step), :]
        for y in range(groups):
            out[y, pl.ds(s * step, step), :] = tile
        edge = near[pl.ds(pl.multiple_of(side * length + nblocks * step, 16), 16), :].astype(F32)
        line = jnp.sum(jnp.where(position == b, edge, 0.0), axis=0, keepdims=True)
        diagonals = jnp.where(position == s, line, diagonals)
    for y in range(groups):
        out[y, pl.ds(slots * step, 16), :] = diagonals.astype(BF16)


def group_kernel(parts, keep, received, out):
    me = lax.axis_index("yh")
    total = keep[me] + received[me].astype(F32)
    for y in range(parts.shape[0]):
        total = total + jnp.where(me == y, 0.0, parts[y].astype(F32))
    out[...] = total.astype(BF16)


def grid_kernel(slots, count, own, other, values, out):
    row, col = iotas()
    upper, lower, middle = [
        jnp.where(mask, 1.0, 0.0).astype(BF16) for mask in (col >= row, col < row, col == row)
    ]
    first_core = lax.axis_index("core") == 0
    groups = own.shape[0]
    step = HALF // groups
    total = jnp.zeros(values.shape[1:], F32)
    lines = own[0, pl.ds(slots * step, 16), :].astype(F32)
    for s in range(slots):
        at = pl.ds(s * step, step)
        mine = jnp.concatenate([own[y, at, :] for y in range(groups)], axis=0)
        theirs = jnp.concatenate([other[y, at, :] for y in range(groups)], axis=0)
        first = jnp.where(first_core, mine, theirs)
        second = jnp.where(first_core, theirs, mine)
        line = jnp.broadcast_to(lines[s : s + 1], (HALF, HALF)).astype(BF16)
        top = jnp.concatenate([first * upper, second], axis=1)
        bottom = jnp.concatenate([jnp.zeros_like(first), first * lower + line * middle], axis=1)
        v = values[s]
        inner = dot(v, jnp.concatenate([top, bottom], axis=0))
        total = total + jnp.where(s < count[0], v.astype(F32) * inner, 0.0)
    narrow = total[:, :HALF] + total[:, HALF:]
    for k in range(narrow.shape[0] // HALF):
        piece = narrow[k * HALF : (k + 1) * HALF].T
        out[:, k * HALF : (k + 1) * HALF] = jnp.sum(piece, axis=0, keepdims=True)


def call(kernel, out_shape, in_specs, scratch=(), flops=0, moved=0, vmem=8):
    out_specs = jax.tree.map(lambda _: VMEM, out_shape)
    return pl.pallas_call(
        kernel,
        out_shape=out_shape,
        in_specs=in_specs,
        out_specs=out_specs,
        scratch_shapes=list(scratch),
        compiler_params=pltpu.CompilerParams(vmem_limit_bytes=vmem << 20),
        cost_estimate=pl.CostEstimate(flops=flops, bytes_accessed=moved, transcendentals=0),
    )


def shape(dims, dtype):
    return jax.ShapeDtypeStruct(dims, dtype)


def shards(
    diag_inverse,
    coupling,
    ancestor_inverse,
    pole_weight,
    ancestor_bit,
    tile_blocks,
    tile_count,
    orbital_values,
):
    diag, link, own_upper = diag_inverse[0], coupling[0], ancestor_inverse[0, 0]
    nblocks, slots = diag.shape[0], orbital_values.shape[1]
    nsep, groups = lax.axis_size("sep"), lax.axis_size("yh")
    swap = [(0, 1), (1, 0)]

    order = (2, 0, 3, 1)
    uppers = [lax.ppermute(own_upper, "sep", [(i, i ^ 1 << k) for i in range(nsep)]) for k in order]
    tiles, rows = call(
        lambda *refs: weigh_kernel(nblocks, *refs),
        (shape((nblocks, 2, HALF, HALF), F32), shape((nblocks, HALF), F32)),
        [SMEM, VMEM],
        flops=2_000_000,
        moved=3_200_000,
    )(pole_weight, diag)

    step = HALF // groups
    length = nblocks * step + 16
    keep, send = call(
        lambda *refs: term_kernel(nblocks, order, *refs),
        (shape((groups, length, HALF), F32), shape((groups, length, HALF), BF16)),
        [SMEM, SMEM] + [VMEM] * (3 + LEVELS),
        [pltpu.VMEM((LEVELS, 2, 256, 512), BF16)],
        flops=2_100_000_000,
        moved=5_000_000,
        vmem=16,
    )(ancestor_bit, pole_weight, link, tiles, rows, *uppers)
    received = lax.ppermute(send, "core", swap)
    chip = call(chip_kernel, shape((groups, length, HALF), BF16), [VMEM] * 2, moved=1_400_000)(keep, received)
    parts = lax.all_to_all(chip, "yh", 0, 0, tiled=True)
    held = call(group_kernel, shape((length, HALF), BF16), [VMEM] * 3, moved=600_000)(parts, keep, received)

    before = lax.ppermute(held, "sep", [(i, i + 1) for i in range(nsep - 1)])
    after = lax.ppermute(held, "sep", [(i + 1, i) for i in range(nsep - 1)])
    picked = call(
        lambda *refs: pick_kernel(nblocks, slots, *refs),
        shape((groups, slots * step + 16, HALF), BF16),
        [SMEM] + [VMEM] * 3,
        [pltpu.VMEM((3 * length, HALF), BF16)],
        moved=500_000,
    )(tile_blocks, before, held, after)
    own = lax.all_to_all(picked, "yh", 0, 0, tiled=True)
    other = lax.ppermute(own, "core", swap)
    return call(
        lambda *refs: grid_kernel(slots, *refs),
        shape((1, orbital_values.shape[2]), F32),
        [SMEM] + [VMEM] * 3,
        flops=200_000_000,
        moved=1_300_000,
    )(tile_count, own, other, orbital_values[0])


def solution(mesh):
    pole, sep = mesh.shape["pole"], mesh.shape["sep"]
    split = Mesh(mesh.devices.reshape(pole // 2, 2, sep), ("yh", "core", "sep"))
    poles = ("yh", "core")
    placed = (
        P(poles, "sep", None, None, None),
        P(poles, "sep", None, None, None),
        P(poles, "sep", None, None, None),
        P(poles, None),
        P("sep"),
        P("sep", None),
        P("sep"),
        P("sep", None, poles, None),
    )
    return jax.shard_map(shards, mesh=split, in_specs=placed, out_specs=P("sep", poles), check_vma=False)
```

```python
import jax
import jax.numpy as jnp
from jax import lax
from jax.experimental import pallas as pl
from jax.experimental.pallas import tpu as pltpu
from jax.sharding import Mesh, PartitionSpec as P

LEVELS = 4
HALF = 128
F32 = jnp.float32
BF16 = jnp.bfloat16
SMEM = pl.BlockSpec(memory_space=pltpu.SMEM)
VMEM = pl.BlockSpec(memory_space=pltpu.VMEM)


def iotas():
    row = lax.broadcasted_iota(jnp.int32, (HALF, HALF), 0)
    col = lax.broadcasted_iota(jnp.int32, (HALF, HALF), 1)
    return row, col


def packed(t):
    row, col = iotas()
    t00, t01 = t[:HALF, :HALF], t[:HALF, HALF:]
    t10, t11 = t[HALF:, :HALF], t[HALF:, HALF:]
    here = jnp.where(col >= row, t00, t11)
    there = jnp.where(col > row, t11, jnp.where(col < row, t00, 0.0))
    diagonal = jnp.sum(jnp.where(col == row, t11, 0.0), axis=0, keepdims=True)
    return here + there.T, t01 + t10.T, diagonal


def weigh_kernel(nblocks, weight, diag, tiles, rows):
    for b in range(nblocks):
        t = weight[0, 0] * diag[b, 1].astype(F32) + weight[0, 1] * diag[b, 0].astype(F32)
        first, second, diagonal = packed(t)
        tiles[b, 0] = first
        tiles[b, 1] = second
        rows[pl.ds(b, 1), :] = diagonal


def dot(left, right):
    return lax.dot_general(left, right, (((1,), (0,)), ((), ())), preferred_element_type=F32)


def dot_t(left, right):
    return lax.dot_general(left, right, (((1,), (1,)), ((), ())), preferred_element_type=F32)


def term_kernel(nblocks, order, bit, weight, link, tiles, rows, *refs):
    uppers, (keep, send, pair) = refs[: len(order)], refs[len(order) :]
    for level, up in zip(order, uppers):
        pair[level, 0, :, :256] = up[0]
        pair[level, 0, :, 256:] = up[1]
        pair[level, 1, :, :256] = -up[1]
        pair[level, 1, :, 256:] = up[0]
    first_core = lax.axis_index("core") == 0
    groups = keep.shape[0]
    step = HALF // groups
    for b in range(nblocks):
        level = bit[b]
        lr, li = link[b, 0], link[b, 1]
        middle = (dot(lr, pair[level, 0]) + dot(li, pair[level, 1])).astype(BF16)
        mr, mi = middle[:, :256], middle[:, 256:]
        real = dot_t(mr, lr) - dot_t(mi, li)
        imag = dot_t(mr, li) + dot_t(mi, lr)
        first, second, diagonal = packed(weight[0, 0] * imag + weight[0, 1] * real)
        first = first + tiles[b, 0]
        second = second + tiles[b, 1]
        mine = jnp.where(first_core, first, second)
        theirs = jnp.where(first_core, second, first)
        at = pl.ds(b * step, step)
        for y in range(groups):
            keep[y, at, :] = mine[y * step : (y + 1) * step]
            send[y, at, :] = theirs[y * step : (y + 1) * step].astype(BF16)
        keep[0, pl.ds(nblocks * step + b, 1), :] = diagonal + rows[pl.ds(b, 1), :]
    tail = pl.ds(nblocks * step, 16)
    keep[0, pl.ds(nblocks * step + nblocks, 16 - nblocks), :] = jnp.zeros((16 - nblocks, HALF), F32)
    edge = keep[0, tail, :]
    for y in range(groups):
        keep[y, tail, :] = edge
        send[y, tail, :] = edge.astype(BF16)


def chip_kernel(mine, theirs, out):
    out[...] = (mine[...] + theirs[...].astype(F32)).astype(BF16)


def pick_kernel(nblocks, slots, listed, across, own, within, out, near):
    groups, length = out.shape[0], own.shape[0]
    step = HALF // groups
    base = (lax.axis_index("sep") - 1) * nblocks
    position = lax.broadcasted_iota(jnp.int32, (16, HALF), 0)
    odd = lax.axis_index("sep") % 2 == 1
    near[pl.ds(0, length), :] = jnp.where(odd, within[...], across[...])
    near[pl.ds(length, length), :] = own[...]
    near[pl.ds(2 * length, length), :] = jnp.where(odd, across[...], within[...])
    diagonals = jnp.zeros((16, HALF), F32)
    for s in range(slots):
        where = listed[0, s] - base
        side, b = where // nblocks, where % nblocks
        tile = near[pl.ds(pl.multiple_of(side * length + b * step, 16), step), :]
        for y in range(groups):
            out[y, pl.ds(s * step, step), :] = tile
        edge = near[pl.ds(pl.multiple_of(side * length + nblocks * step, 16), 16), :].astype(F32)
        line = jnp.sum(jnp.where(position == b, edge, 0.0), axis=0, keepdims=True)
        diagonals = jnp.where(position == s, line, diagonals)
    for y in range(groups):
        out[y, pl.ds(slots * step, 16), :] = diagonals.astype(BF16)


def group_kernel(parts, keep, received, out):
    me = lax.axis_index("yh")
    total = keep[me] + received[me].astype(F32)
    for y in range(parts.shape[0]):
        total = total + jnp.where(me == y, 0.0, parts[y].astype(F32))
    out[...] = total.astype(BF16)


def grid_kernel(slots, count, own, other, values, out):
    row, col = iotas()
    upper, lower, middle = [
        jnp.where(mask, 1.0, 0.0).astype(BF16) for mask in (col >= row, col < row, col == row)
    ]
    first_core = lax.axis_index("core") == 0
    groups = own.shape[0]
    step = HALF // groups
    total = jnp.zeros(values.shape[1:], F32)
    lines = own[0, pl.ds(slots * step, 16), :].astype(F32)
    for s in range(slots):
        at = pl.ds(s * step, step)
        mine = jnp.concatenate([own[y, at, :] for y in range(groups)], axis=0)
        theirs = jnp.concatenate([other[y, at, :] for y in range(groups)], axis=0)
        first = jnp.where(first_core, mine, theirs)
        second = jnp.where(first_core, theirs, mine)
        line = jnp.broadcast_to(lines[s : s + 1], (HALF, HALF)).astype(BF16)
        top = jnp.concatenate([first * upper, second], axis=1)
        bottom = jnp.concatenate([jnp.zeros_like(first), first * lower + line * middle], axis=1)
        v = values[s]
        inner = dot(v, jnp.concatenate([top, bottom], axis=0))
        total = total + jnp.where(s < count[0], v.astype(F32) * inner, 0.0)
    narrow = total[:, :HALF] + total[:, HALF:]
    for k in range(narrow.shape[0] // HALF):
        piece = narrow[k * HALF : (k + 1) * HALF].T
        out[:, k * HALF : (k + 1) * HALF] = jnp.sum(piece, axis=0, keepdims=True)


def call(kernel, out_shape, in_specs, scratch=(), flops=0, moved=0, vmem=8):
    out_specs = jax.tree.map(lambda _: VMEM, out_shape)
    return pl.pallas_call(
        kernel,
        out_shape=out_shape,
        in_specs=in_specs,
        out_specs=out_specs,
        scratch_shapes=list(scratch),
        compiler_params=pltpu.CompilerParams(vmem_limit_bytes=vmem << 20),
        cost_estimate=pl.CostEstimate(flops=flops, bytes_accessed=moved, transcendentals=0),
    )


def shape(dims, dtype):
    return jax.ShapeDtypeStruct(dims, dtype)


def shards(
    diag_inverse,
    coupling,
    ancestor_inverse,
    pole_weight,
    ancestor_bit,
    tile_blocks,
    tile_count,
    orbital_values,
):
    diag, link, own_upper = diag_inverse[0], coupling[0], ancestor_inverse[0, 0]
    nblocks, slots = diag.shape[0], orbital_values.shape[1]
    nsep, groups = lax.axis_size("sep"), lax.axis_size("yh")
    swap = [(0, 1), (1, 0)]

    order = (2, 0, 3, 1)
    uppers = [lax.ppermute(own_upper, "sep", [(i, i ^ 1 << k) for i in range(nsep)]) for k in order]
    tiles, rows = call(
        lambda *refs: weigh_kernel(nblocks, *refs),
        (shape((nblocks, 2, HALF, HALF), F32), shape((nblocks, HALF), F32)),
        [SMEM, VMEM],
        flops=2_000_000,
        moved=3_200_000,
    )(pole_weight, diag)

    step = HALF // groups
    length = nblocks * step + 16
    keep, send = call(
        lambda *refs: term_kernel(nblocks, order, *refs),
        (shape((groups, length, HALF), F32), shape((groups, length, HALF), BF16)),
        [SMEM, SMEM] + [VMEM] * (3 + LEVELS),
        [pltpu.VMEM((LEVELS, 2, 256, 512), BF16)],
        flops=2_100_000_000,
        moved=5_000_000,
        vmem=16,
    )(ancestor_bit, pole_weight, link, tiles, rows, *uppers)
    received = lax.ppermute(send, "core", swap)
    chip = call(chip_kernel, shape((groups, length, HALF), BF16), [VMEM] * 2, moved=1_400_000)(keep, received)
    parts = lax.all_to_all(chip, "yh", 0, 0, tiled=True)
    held = call(group_kernel, shape((length, HALF), BF16), [VMEM] * 3, moved=600_000)(parts, keep, received)

    odd = range(1, nsep - 1, 2)
    across = lax.ppermute(held, "sep", [(i, i + 1) for i in odd] + [(i + 1, i) for i in odd])
    within = lax.ppermute(held, "sep", [(i, i ^ 1) for i in range(nsep)])
    picked = call(
        lambda *refs: pick_kernel(nblocks, slots, *refs),
        shape((groups, slots * step + 16, HALF), BF16),
        [SMEM] + [VMEM] * 3,
        [pltpu.VMEM((3 * length, HALF), BF16)],
        moved=500_000,
    )(tile_blocks, across, held, within)
    own = lax.all_to_all(picked, "yh", 0, 0, tiled=True)
    other = lax.ppermute(own, "core", swap)
    return call(
        lambda *refs: grid_kernel(slots, *refs),
        shape((1, orbital_values.shape[2]), F32),
        [SMEM] + [VMEM] * 3,
        flops=200_000_000,
        moved=1_300_000,
    )(tile_count, own, other, orbital_values[0])


def solution(mesh):
    pole, sep = mesh.shape["pole"], mesh.shape["sep"]
    split = Mesh(mesh.devices.reshape(pole // 2, 2, sep), ("yh", "core", "sep"))
    poles = ("yh", "core")
    placed = (
        P(poles, "sep", None, None, None),
        P(poles, "sep", None, None, None),
        P(poles, "sep", None, None, None),
        P(poles, None),
        P("sep"),
        P("sep", None),
        P("sep"),
        P("sep", None, poles, None),
    )
    return jax.shard_map(shards, mesh=split, in_specs=placed, out_specs=P("sep", poles), check_vma=False)
```

```python
import jax
import jax.numpy as jnp
from jax import lax
from jax.experimental import pallas as pl
from jax.experimental.pallas import tpu as pltpu
from jax.sharding import Mesh, PartitionSpec as P

LEVELS = 4
HALF = 128
F32 = jnp.float32
BF16 = jnp.bfloat16
SMEM = pl.BlockSpec(memory_space=pltpu.SMEM)
VMEM = pl.BlockSpec(memory_space=pltpu.VMEM)


def iotas():
    row = lax.broadcasted_iota(jnp.int32, (HALF, HALF), 0)
    col = lax.broadcasted_iota(jnp.int32, (HALF, HALF), 1)
    return row, col


def packed(t):
    row, col = iotas()
    t00, t01 = t[:HALF, :HALF], t[:HALF, HALF:]
    t10, t11 = t[HALF:, :HALF], t[HALF:, HALF:]
    here = jnp.where(col >= row, t00, t11)
    there = jnp.where(col > row, t11, jnp.where(col < row, t00, 0.0))
    diagonal = jnp.sum(jnp.where(col == row, t11, 0.0), axis=0, keepdims=True)
    return here + there.T, t01 + t10.T, diagonal


def weigh_kernel(nblocks, weight, diag, tiles, rows):
    for b in range(nblocks):
        t = weight[0, 0] * diag[b, 1].astype(F32) + weight[0, 1] * diag[b, 0].astype(F32)
        first, second, diagonal = packed(t)
        tiles[b, 0] = first
        tiles[b, 1] = second
        rows[pl.ds(b, 1), :] = diagonal


def dot(left, right):
    return lax.dot_general(left, right, (((1,), (0,)), ((), ())), preferred_element_type=F32)


def dot_t(left, right):
    return lax.dot_general(left, right, (((1,), (1,)), ((), ())), preferred_element_type=F32)


def term_kernel(nblocks, order, bit, weight, link, tiles, rows, *refs):
    uppers, (keep, send, pair) = refs[: len(order)], refs[len(order) :]
    for level, up in zip(order, uppers):
        pair[level, 0, :, :256] = up[0]
        pair[level, 0, :, 256:] = up[1]
        pair[level, 1, :, :256] = -up[1]
        pair[level, 1, :, 256:] = up[0]
    first_core = lax.axis_index("core") == 0
    groups = keep.shape[0]
    step = HALF // groups
    for b in range(nblocks):
        level = bit[b]
        lr, li = link[b, 0], link[b, 1]
        middle = (dot(lr, pair[level, 0]) + dot(li, pair[level, 1])).astype(BF16)
        mr, mi = middle[:, :256], middle[:, 256:]
        real = dot_t(mr, lr) - dot_t(mi, li)
        imag = dot_t(mr, li) + dot_t(mi, lr)
        first, second, diagonal = packed(weight[0, 0] * imag + weight[0, 1] * real)
        first = first + tiles[b, 0]
        second = second + tiles[b, 1]
        mine = jnp.where(first_core, first, second)
        theirs = jnp.where(first_core, second, first)
        at = pl.ds(b * step, step)
        for y in range(groups):
            keep[y, at, :] = mine[y * step : (y + 1) * step]
            send[y, at, :] = theirs[y * step : (y + 1) * step].astype(BF16)
        keep[0, pl.ds(nblocks * step + b, 1), :] = diagonal + rows[pl.ds(b, 1), :]
    tail = pl.ds(nblocks * step, 16)
    keep[0, pl.ds(nblocks * step + nblocks, 16 - nblocks), :] = jnp.zeros((16 - nblocks, HALF), F32)
    edge = keep[0, tail, :]
    for y in range(groups):
        keep[y, tail, :] = edge
        send[y, tail, :] = edge.astype(BF16)


def chip_kernel(mine, theirs, out):
    out[...] = (mine[...] + theirs[...].astype(F32)).astype(BF16)


def pick_kernel(nblocks, slots, listed, within, own, across, out, near):
    groups, length = out.shape[0], own.shape[0]
    step = HALF // groups
    base = (lax.axis_index("sep") - 1) * nblocks
    position = lax.broadcasted_iota(jnp.int32, (16, HALF), 0)
    odd = lax.axis_index("sep") % 2 == 1
    near[pl.ds(0, length), :] = jnp.where(odd, within[...], across[...])
    near[pl.ds(length, length), :] = own[...]
    near[pl.ds(2 * length, length), :] = jnp.where(odd, across[...], within[...])
    diagonals = jnp.zeros((16, HALF), F32)
    for s in range(slots):
        where = listed[0, s] - base
        side, b = where // nblocks, where % nblocks
        tile = near[pl.ds(pl.multiple_of(side * length + b * step, 16), step), :]
        for y in range(groups):
            out[y, pl.ds(s * step, step), :] = tile
        edge = near[pl.ds(pl.multiple_of(side * length + nblocks * step, 16), 16), :].astype(F32)
        line = jnp.sum(jnp.where(position == b, edge, 0.0), axis=0, keepdims=True)
        diagonals = jnp.where(position == s, line, diagonals)
    for y in range(groups):
        out[y, pl.ds(slots * step, 16), :] = diagonals.astype(BF16)


def group_kernel(parts, keep, received, out):
    me = lax.axis_index("yh")
    total = keep[me] + received[me].astype(F32)
    for y in range(parts.shape[0]):
        total = total + jnp.where(me == y, 0.0, parts[y].astype(F32))
    out[...] = total.astype(BF16)


def grid_kernel(slots, count, own, other, values, out):
    row, col = iotas()
    upper, lower, middle = [
        jnp.where(mask, 1.0, 0.0).astype(BF16) for mask in (col >= row, col < row, col == row)
    ]
    first_core = lax.axis_index("core") == 0
    groups = own.shape[0]
    step = HALF // groups
    total = jnp.zeros(values.shape[1:], F32)
    lines = own[0, pl.ds(slots * step, 16), :].astype(F32)
    for s in range(slots):
        at = pl.ds(s * step, step)
        mine = jnp.concatenate([own[y, at, :] for y in range(groups)], axis=0)
        theirs = jnp.concatenate([other[y, at, :] for y in range(groups)], axis=0)
        first = jnp.where(first_core, mine, theirs)
        second = jnp.where(first_core, theirs, mine)
        line = jnp.broadcast_to(lines[s : s + 1], (HALF, HALF)).astype(BF16)
        top = jnp.concatenate([first * upper, second], axis=1)
        bottom = jnp.concatenate([jnp.zeros_like(first), first * lower + line * middle], axis=1)
        v = values[s]
        inner = dot(v, jnp.concatenate([top, bottom], axis=0))
        total = total + jnp.where(s < count[0], v.astype(F32) * inner, 0.0)
    narrow = total[:, :HALF] + total[:, HALF:]
    for k in range(narrow.shape[0] // HALF):
        piece = narrow[k * HALF : (k + 1) * HALF].T
        out[:, k * HALF : (k + 1) * HALF] = jnp.sum(piece, axis=0, keepdims=True)


def call(kernel, out_shape, in_specs, scratch=(), flops=0, moved=0, vmem=8):
    out_specs = jax.tree.map(lambda _: VMEM, out_shape)
    return pl.pallas_call(
        kernel,
        out_shape=out_shape,
        in_specs=in_specs,
        out_specs=out_specs,
        scratch_shapes=list(scratch),
        compiler_params=pltpu.CompilerParams(vmem_limit_bytes=vmem << 20),
        cost_estimate=pl.CostEstimate(flops=flops, bytes_accessed=moved, transcendentals=0),
    )


def shape(dims, dtype):
    return jax.ShapeDtypeStruct(dims, dtype)


def shards(
    diag_inverse,
    coupling,
    ancestor_inverse,
    pole_weight,
    ancestor_bit,
    tile_blocks,
    tile_count,
    orbital_values,
):
    diag, link, own_upper = diag_inverse[0], coupling[0], ancestor_inverse[0, 0]
    nblocks, slots = diag.shape[0], orbital_values.shape[1]
    nsep, groups = lax.axis_size("sep"), lax.axis_size("yh")
    swap = [(0, 1), (1, 0)]

    order = (2, 0, 3, 1)
    uppers = [lax.ppermute(own_upper, "sep", [(i, i ^ 1 << k) for i in range(nsep)]) for k in order]
    tiles, rows = call(
        lambda *refs: weigh_kernel(nblocks, *refs),
        (shape((nblocks, 2, HALF, HALF), F32), shape((nblocks, HALF), F32)),
        [SMEM, VMEM],
        flops=2_000_000,
        moved=3_200_000,
    )(pole_weight, diag)

    step = HALF // groups
    length = nblocks * step + 16
    keep, send = call(
        lambda *refs: term_kernel(nblocks, order, *refs),
        (shape((groups, length, HALF), F32), shape((groups, length, HALF), BF16)),
        [SMEM, SMEM] + [VMEM] * (3 + LEVELS),
        [pltpu.VMEM((LEVELS, 2, 256, 512), BF16)],
        flops=2_100_000_000,
        moved=5_000_000,
        vmem=16,
    )(ancestor_bit, pole_weight, link, tiles, rows, *uppers)
    received = lax.ppermute(send, "core", swap)
    chip = call(chip_kernel, shape((groups, length, HALF), BF16), [VMEM] * 2, moved=1_400_000)(keep, received)
    parts = lax.all_to_all(chip, "yh", 0, 0, tiled=True)
    held = call(group_kernel, shape((length, HALF), BF16), [VMEM] * 3, moved=600_000)(parts, keep, received)

    odd = range(1, nsep - 1, 2)
    within = lax.ppermute(held, "sep", [(i, i ^ 1) for i in range(nsep)])
    across = lax.ppermute(held, "sep", [(i, i + 1) for i in odd] + [(i + 1, i) for i in odd])
    picked = call(
        lambda *refs: pick_kernel(nblocks, slots, *refs),
        shape((groups, slots * step + 16, HALF), BF16),
        [SMEM] + [VMEM] * 3,
        [pltpu.VMEM((3 * length, HALF), BF16)],
        moved=500_000,
    )(tile_blocks, within, held, across)
    own = lax.all_to_all(picked, "yh", 0, 0, tiled=True)
    other = lax.ppermute(own, "core", swap)
    return call(
        lambda *refs: grid_kernel(slots, *refs),
        shape((1, orbital_values.shape[2]), F32),
        [SMEM] + [VMEM] * 3,
        flops=200_000_000,
        moved=1_300_000,
    )(tile_count, own, other, orbital_values[0])


def solution(mesh):
    pole, sep = mesh.shape["pole"], mesh.shape["sep"]
    split = Mesh(mesh.devices.reshape(pole // 2, 2, sep), ("yh", "core", "sep"))
    poles = ("yh", "core")
    placed = (
        P(poles, "sep", None, None, None),
        P(poles, "sep", None, None, None),
        P(poles, "sep", None, None, None),
        P(poles, None),
        P("sep"),
        P("sep", None),
        P("sep"),
        P("sep", None, poles, None),
    )
    return jax.shard_map(shards, mesh=split, in_specs=placed, out_specs=P("sep", poles), check_vma=False)
```

```python
import jax
import jax.numpy as jnp
from jax import lax
from jax.experimental import pallas as pl
from jax.experimental.pallas import tpu as pltpu
from jax.sharding import Mesh, PartitionSpec as P

LEVELS = 4
HALF = 128
F32 = jnp.float32
BF16 = jnp.bfloat16
SMEM = pl.BlockSpec(memory_space=pltpu.SMEM)
VMEM = pl.BlockSpec(memory_space=pltpu.VMEM)


def iotas():
    row = lax.broadcasted_iota(jnp.int32, (HALF, HALF), 0)
    col = lax.broadcasted_iota(jnp.int32, (HALF, HALF), 1)
    return row, col


def packed(t):
    row, col = iotas()
    t00, t01 = t[:HALF, :HALF], t[:HALF, HALF:]
    t10, t11 = t[HALF:, :HALF], t[HALF:, HALF:]
    here = jnp.where(col >= row, t00, t11)
    there = jnp.where(col > row, t11, jnp.where(col < row, t00, 0.0))
    diagonal = jnp.sum(jnp.where(col == row, t11, 0.0), axis=0, keepdims=True)
    return here + there.T, t01 + t10.T, diagonal


def weigh_kernel(nblocks, weight, diag, tiles, rows):
    for b in range(nblocks):
        t = weight[0, 0] * diag[b, 1].astype(F32) + weight[0, 1] * diag[b, 0].astype(F32)
        first, second, diagonal = packed(t)
        tiles[b, 0] = first
        tiles[b, 1] = second
        rows[pl.ds(b, 1), :] = diagonal


def dot(left, right):
    return lax.dot_general(left, right, (((1,), (0,)), ((), ())), preferred_element_type=F32)


def dot_t(left, right):
    return lax.dot_general(left, right, (((1,), (1,)), ((), ())), preferred_element_type=F32)


def term_kernel(nblocks, order, bit, weight, link, tiles, rows, *refs):
    uppers, (keep, send, pair) = refs[: len(order)], refs[len(order) :]
    for level, up in zip(order, uppers):
        pair[level, 0, :, :256] = up[0]
        pair[level, 0, :, 256:] = up[1]
        pair[level, 1, :, :256] = -up[1]
        pair[level, 1, :, 256:] = up[0]
    first_core = lax.axis_index("core") == 0
    groups = keep.shape[0]
    step = HALF // groups
    for b in range(nblocks):
        level = bit[b]
        lr, li = link[b, 0], link[b, 1]
        middle = (dot(lr, pair[level, 0]) + dot(li, pair[level, 1])).astype(BF16)
        mr, mi = middle[:, :256], middle[:, 256:]
        real = dot_t(mr, lr) - dot_t(mi, li)
        imag = dot_t(mr, li) + dot_t(mi, lr)
        first, second, diagonal = packed(weight[0, 0] * imag + weight[0, 1] * real)
        first = first + tiles[b, 0]
        second = second + tiles[b, 1]
        mine = jnp.where(first_core, first, second)
        theirs = jnp.where(first_core, second, first)
        at = pl.ds(b * step, step)
        for y in range(groups):
            keep[y, at, :] = mine[y * step : (y + 1) * step]
            send[y, at, :] = theirs[y * step : (y + 1) * step].astype(BF16)
        keep[0, pl.ds(nblocks * step + b, 1), :] = diagonal + rows[pl.ds(b, 1), :]
    tail = pl.ds(nblocks * step, 16)
    keep[0, pl.ds(nblocks * step + nblocks, 16 - nblocks), :] = jnp.zeros((16 - nblocks, HALF), F32)
    edge = keep[0, tail, :]
    for y in range(groups):
        keep[y, tail, :] = edge
        send[y, tail, :] = edge.astype(BF16)


def chip_kernel(mine, theirs, out):
    out[...] = (mine[...] + theirs[...].astype(F32)).astype(BF16)


def pick_kernel(nblocks, slots, listed, before, own, after, out, near):
    groups, length = out.shape[0], own.shape[0]
    step = HALF // groups
    base = (lax.axis_index("sep") - 1) * nblocks
    position = lax.broadcasted_iota(jnp.int32, (16, HALF), 0)
    for k, source in enumerate((before, own, after)):
        near[pl.ds(k * length, length), :] = source[...]
    diagonals = jnp.zeros((16, HALF), F32)
    for s in range(slots):
        where = listed[0, s] - base
        side, b = where // nblocks, where % nblocks
        tile = near[pl.ds(pl.multiple_of(side * length + b * step, 16), step), :]
        for y in range(groups):
            out[y, pl.ds(s * step, step), :] = tile
        edge = near[pl.ds(pl.multiple_of(side * length + nblocks * step, 16), 16), :].astype(F32)
        line = jnp.sum(jnp.where(position == b, edge, 0.0), axis=0, keepdims=True)
        diagonals = jnp.where(position == s, line, diagonals)
    for y in range(groups):
        out[y, pl.ds(slots * step, 16), :] = diagonals.astype(BF16)


def group_kernel(parts, keep, received, out):
    me = lax.axis_index("yh")
    total = keep[me] + received[me].astype(F32)
    for y in range(parts.shape[0]):
        total = total + jnp.where(me == y, 0.0, parts[y].astype(F32))
    out[...] = total.astype(BF16)


def grid_kernel(slots, count, own, other, values, out):
    row, col = iotas()
    upper, lower, middle = [
        jnp.where(mask, 1.0, 0.0).astype(BF16) for mask in (col >= row, col < row, col == row)
    ]
    first_core = lax.axis_index("core") == 0
    groups = own.shape[0]
    step = HALF // groups
    total = jnp.zeros(values.shape[1:], F32)
    lines = own[0, pl.ds(slots * step, 16), :].astype(F32)
    for s in range(slots):
        at = pl.ds(s * step, step)
        mine = jnp.concatenate([own[y, at, :] for y in range(groups)], axis=0)
        theirs = jnp.concatenate([other[y, at, :] for y in range(groups)], axis=0)
        first = jnp.where(first_core, mine, theirs)
        second = jnp.where(first_core, theirs, mine)
        line = jnp.broadcast_to(lines[s : s + 1], (HALF, HALF)).astype(BF16)
        top = jnp.concatenate([first * upper, second], axis=1)
        bottom = jnp.concatenate([jnp.zeros_like(first), first * lower + line * middle], axis=1)
        v = values[s]
        inner = dot(v, jnp.concatenate([top, bottom], axis=0))
        total = total + jnp.where(s < count[0], v.astype(F32) * inner, 0.0)
    narrow = total[:, :HALF] + total[:, HALF:]
    for k in range(narrow.shape[0] // HALF):
        piece = narrow[k * HALF : (k + 1) * HALF].T
        out[:, k * HALF : (k + 1) * HALF] = jnp.sum(piece, axis=0, keepdims=True)


def call(kernel, out_shape, in_specs, scratch=(), flops=0, moved=0, vmem=8):
    out_specs = jax.tree.map(lambda _: VMEM, out_shape)
    return pl.pallas_call(
        kernel,
        out_shape=out_shape,
        in_specs=in_specs,
        out_specs=out_specs,
        scratch_shapes=list(scratch),
        compiler_params=pltpu.CompilerParams(vmem_limit_bytes=vmem << 20),
        cost_estimate=pl.CostEstimate(flops=flops, bytes_accessed=moved, transcendentals=0),
    )


def shape(dims, dtype):
    return jax.ShapeDtypeStruct(dims, dtype)


def shards(
    diag_inverse,
    coupling,
    ancestor_inverse,
    pole_weight,
    ancestor_bit,
    tile_blocks,
    tile_count,
    orbital_values,
):
    diag, link, own_upper = diag_inverse[0], coupling[0], ancestor_inverse[0, 0]
    nblocks, slots = diag.shape[0], orbital_values.shape[1]
    nsep, groups = lax.axis_size("sep"), lax.axis_size("yh")
    swap = [(0, 1), (1, 0)]

    order = (3, 0, 2, 1)
    uppers = [lax.ppermute(own_upper, "sep", [(i, i ^ 1 << k) for i in range(nsep)]) for k in order]
    tiles, rows = call(
        lambda *refs: weigh_kernel(nblocks, *refs),
        (shape((nblocks, 2, HALF, HALF), F32), shape((nblocks, HALF), F32)),
        [SMEM, VMEM],
        flops=2_000_000,
        moved=3_200_000,
    )(pole_weight, diag)

    step = HALF // groups
    length = nblocks * step + 16
    keep, send = call(
        lambda *refs: term_kernel(nblocks, order, *refs),
        (shape((groups, length, HALF), F32), shape((groups, length, HALF), BF16)),
        [SMEM, SMEM] + [VMEM] * (3 + LEVELS),
        [pltpu.VMEM((LEVELS, 2, 256, 512), BF16)],
        flops=2_100_000_000,
        moved=5_000_000,
        vmem=16,
    )(ancestor_bit, pole_weight, link, tiles, rows, *uppers)
    received = lax.ppermute(send, "core", swap)
    chip = call(chip_kernel, shape((groups, length, HALF), BF16), [VMEM] * 2, moved=1_400_000)(keep, received)
    parts = lax.all_to_all(chip, "yh", 0, 0, tiled=True)
    held = call(group_kernel, shape((length, HALF), BF16), [VMEM] * 3, moved=600_000)(parts, keep, received)

    before = lax.ppermute(held, "sep", [(i, i + 1) for i in range(nsep - 1)])
    after = lax.ppermute(held, "sep", [(i + 1, i) for i in range(nsep - 1)])
    picked = call(
        lambda *refs: pick_kernel(nblocks, slots, *refs),
        shape((groups, slots * step + 16, HALF), BF16),
        [SMEM] + [VMEM] * 3,
        [pltpu.VMEM((3 * length, HALF), BF16)],
        moved=500_000,
    )(tile_blocks, before, held, after)
    own = lax.all_to_all(picked, "yh", 0, 0, tiled=True)
    other = lax.ppermute(own, "core", swap)
    return call(
        lambda *refs: grid_kernel(slots, *refs),
        shape((1, orbital_values.shape[2]), F32),
        [SMEM] + [VMEM] * 3,
        flops=200_000_000,
        moved=1_300_000,
    )(tile_count, own, other, orbital_values[0])


def solution(mesh):
    pole, sep = mesh.shape["pole"], mesh.shape["sep"]
    split = Mesh(mesh.devices.reshape(pole // 2, 2, sep), ("yh", "core", "sep"))
    poles = ("yh", "core")
    placed = (
        P(poles, "sep", None, None, None),
        P(poles, "sep", None, None, None),
        P(poles, "sep", None, None, None),
        P(poles, None),
        P("sep"),
        P("sep", None),
        P("sep"),
        P("sep", None, poles, None),
    )
    return jax.shard_map(shards, mesh=split, in_specs=placed, out_specs=P("sep", poles), check_vma=False)
```
